32 devices in a mesh: row: 8 (over y, x, core), col: 4 (over z).
Axes of the slice: x: 2, y: 2, z: 4, core: 2. Of those that a mesh axis runs over, the one named last changes fastest.
Arguments:
- multispectral: float32 [8, 256, 512], P('col', 'row'), may hold values from -6 to 6
- panchromatic: float32 [1024, 2048], P('row', 'col'), may hold values from -6 to 6
- band_gains: float32 [8, 3], replicated, may hold values from 0.5 to 2
Outputs:
- sharpened: float32 [8, 1024, 2048], P(None, 'row', 'col')
The draws below stay inside these ranges and needn't reach their ends.
All inputs are finite; a program needn't handle non-finite values.
Results may differ from the reference program's by a relative error of at most 0.000065.
Values sent between devices are 32-bit elements; how exact they have to be, the bound alone decides.
No kernel may reach another device: no remote copies, remote signals or barrier semaphores. Data moves between devices by JAX's collectives and lax.ppermute only.
A program may use at most 128 MiB of HBM per device.

```python
import math
import jax
import jax.numpy as jnp
from jax import lax

BANDS = 8
LEVELS = 3
IMG_ROWS = 1024
IMG_COLS = 2048
LOW_ROWS = 256
LOW_COLS = 512


def levels(own_key, shape, split, smallest, high):
    level = 1.0
    for axis_at, shards_of in split:
        draws = jax.random.uniform(jax.random.fold_in(jax.random.fold_in(own_key, 6), axis_at), (shards_of,), jnp.float32, smallest / len(split), high / len(split))
        level = level * jnp.repeat(jnp.exp(draws), shape[axis_at] // shards_of).reshape((-1,) + (1,) * (len(shape) - 1 - axis_at))
    return level


def gaussian(own_key, extent, width, reach, split=(), held_as=jnp.bfloat16):
    entries = width * jax.random.normal(own_key, extent, jnp.float32)
    if split:
        entries = entries * levels(own_key, extent, split, -0.22, 0.18)
    return jnp.clip(entries, -reach, reach).astype(held_as)


def setup_inputs(seed: int = 0) -> dict:
    keys = jax.random.split(jax.random.key(seed), 4)
    return {
        "multispectral": gaussian(keys[0], (BANDS, LOW_ROWS, LOW_COLS), 1.0, 6.0, ((0, 4), (1, 8)), jnp.float32),
        "panchromatic": gaussian(keys[1], (IMG_ROWS, IMG_COLS), 1.0, 6.0, ((0, 8), (1, 4)), jnp.float32),
        "band_gains": jnp.clip(jnp.exp(jax.random.uniform(keys[2], (BANDS, LEVELS), jnp.float32, math.log(0.5), math.log(2.0))), 0.5, 2.0),
    }


daubechies_taps = [0.2303778133088964, 0.7148465705529154, 0.6308807679298587, -0.0279837694168599, -0.1870348117190931, 0.0308413818355607, 0.0328830116668852, -0.0105974017850690]


def tree_filters(tree_index):
    lowpass = list(daubechies_taps) if tree_index == 0 else list(reversed(daubechies_taps))
    highpass = [((-1) ** tap_index) * lowpass[7 - tap_index] for tap_index in range(8)]
    return lowpass, highpass, 3 + tree_index


def cubic_weight(distance):
    magnitude = abs(distance)
    if magnitude <= 1.0:
        return 1.5 * magnitude ** 3 - 2.5 * magnitude ** 2 + 1.0
    if magnitude < 2.0:
        return -0.5 * magnitude ** 3 + 2.5 * magnitude ** 2 - 4.0 * magnitude + 2.0
    return 0.0


def alternate(phase_parts, axis_dim):
    stacked = jnp.stack(phase_parts, axis=axis_dim + 1)
    new_shape = list(phase_parts[0].shape)
    new_shape[axis_dim] = new_shape[axis_dim] * len(phase_parts)
    return stacked.reshape(new_shape)


def upsample_axis(extended, margin, axis_dim):
    out_count = extended.shape[axis_dim] - 4
    phase_parts = []
    for phase_index in range(4):
        position = (phase_index + 0.5) / 4.0 - 0.5
        floor_shift = math.floor(position)
        fraction = position - floor_shift
        summed = None
        for neighbour in (-1, 0, 1, 2):
            first_index = 2 + floor_shift + neighbour
            strided = lax.slice_in_dim(extended, first_index, first_index + out_count, 1, axis_dim)
            term = cubic_weight(fraction - neighbour) * strided
            summed = term if summed is None else summed + term
        phase_parts.append(summed)
    return alternate(phase_parts, axis_dim)


def upsample_tile(extended, margin):
    return upsample_axis(upsample_axis(extended, margin, 1), margin, 2)


def analyze_axis(extended, tap_sets, offset, axis_dim):
    out_count = (extended.shape[axis_dim] - 8) // 2
    results = []
    for tap_weights in tap_sets:
        summed = None
        for tap_index in range(8):
            first_index = 4 - offset + tap_index
            strided = lax.slice_in_dim(extended, first_index, first_index + 2 * out_count - 1, 2, axis_dim)
            term = tap_weights[tap_index] * strided
            summed = term if summed is None else summed + term
        results.append(summed)
    return results


def synthesize_axis(low_ext, high_ext, lowpass, highpass, offset, axis_dim):
    present = [(member, tap_weights) for member, tap_weights in ((low_ext, lowpass), (high_ext, highpass)) if member is not None]
    if len(present) == 0:
        return None
    out_count = present[0][0].shape[axis_dim] - 4
    phase_parts = []
    for parity in (0, 1):
        summed = None
        for member, tap_weights in present:
            for tap_index in range(8):
                if (offset + parity - tap_index) % 2 == 0:
                    first_index = 2 + (offset + parity - tap_index) // 2
                    strided = lax.slice_in_dim(member, first_index, first_index + out_count, 1, axis_dim)
                    term = tap_weights[tap_index] * strided
                    summed = term if summed is None else summed + term
        phase_parts.append(summed)
    return alternate(phase_parts, axis_dim)


def rows_full(col_low, col_high, row_tree):
    lowpass, highpass, offset = tree_filters(row_tree)
    low_low, low_high = analyze_axis(col_low, [lowpass, highpass], offset, 1)
    high_low, high_high = analyze_axis(col_high, [lowpass, highpass], offset, 1)
    return low_low, (low_high, high_low, high_high)


def analyze_full(extended, col_tree, row_tree):
    lowpass, highpass, offset = tree_filters(col_tree)
    col_low, col_high = analyze_axis(extended, [lowpass, highpass], offset, 2)
    return rows_full(col_low, col_high, row_tree)


def analyze_low(extended, col_tree, row_tree):
    col_lowpass, col_highpass, col_offset = tree_filters(col_tree)
    row_lowpass, row_highpass, row_offset = tree_filters(row_tree)
    col_low = analyze_axis(extended, [col_lowpass], col_offset, 2)[0]
    return analyze_axis(col_low, [row_lowpass], row_offset, 1)[0]


def synthesize_tile(low_low, low_high, high_low, high_high, col_tree, row_tree):
    col_lowpass, col_highpass, col_offset = tree_filters(col_tree)
    row_lowpass, row_highpass, row_offset = tree_filters(row_tree)
    col_low = synthesize_axis(low_low, low_high, row_lowpass, row_highpass, row_offset, 1)
    col_high = synthesize_axis(high_low, high_high, row_lowpass, row_highpass, row_offset, 1)
    return synthesize_axis(col_low, col_high, col_lowpass, col_highpass, col_offset, 2)


def wrap_pad(field_stack, rim_width):
    return jnp.pad(field_stack, ((0, 0), (rim_width, rim_width), (rim_width, rim_width)), mode="wrap")


def reference(multispectral, panchromatic, band_gains):
    upsampled = upsample_tile(wrap_pad(multispectral, 2), 2)
    accumulated = jnp.zeros(upsampled.shape, jnp.float32)
    for col_tree in range(2):
        for row_tree in range(2):
            pan_low = panchromatic[None]
            pan_details = []
            for level_index in range(LEVELS):
                pan_low, details = analyze_full(wrap_pad(pan_low, 4), col_tree, row_tree)
                pan_details.append(details)

            def one_band(operands):
                band_field, gains_row = operands
                current = band_field[None]
                for level_index in range(LEVELS):
                    current = analyze_low(wrap_pad(current, 4), col_tree, row_tree)
                for level_index in reversed(range(LEVELS)):
                    merged_bands = [gains_row[level_index] * detail for detail in pan_details[level_index]]
                    padded = [wrap_pad(member, 2) for member in [current] + merged_bands]
                    current = synthesize_tile(padded[0], padded[1], padded[2], padded[3], col_tree, row_tree)
                return current[0]

            accumulated = accumulated + lax.map(one_band, (upsampled, band_gains))
    return 0.25 * accumulated
```

```python
import functools

import jax
import jax.numpy as jnp
import numpy as np
from jax import lax
from jax.experimental import pallas as pl
from jax.experimental.pallas import tpu as pltpu
from jax.sharding import PartitionSpec as P

LEVELS = 3
TAPS = [
    0.2303778133088964,
    0.7148465705529155,
    0.6308807679298587,
    -0.0279837694168599,
    -0.1870348117190931,
    0.0308413818355607,
    0.0328830116668852,
    -0.010597401785069,
]
REACH = 48
COEFS = 24
RIM = 16
BAND_ROWS = 56
VMEM = pltpu.VMEM
F32, BF16 = jnp.float32, jnp.bfloat16


def keys_weight(t):
    t = abs(t)
    if t <= 1.0:
        return 1.5 * t**3 - 2.5 * t**2 + 1.0
    return -0.5 * t**3 + 2.5 * t**2 - 4.0 * t + 2.0 if t < 2.0 else 0.0


def upsample_matrix(n):
    m = np.zeros((n, n // 4))
    for y in range(n):
        centre = (y + 0.5) / 4.0 - 0.5
        for k in range(int(np.floor(centre)) - 1, int(np.floor(centre)) + 3):
            m[y, k % (n // 4)] += keys_weight(centre - k)
    return m


def low_matrix(n, tree):
    taps, offset = (TAPS, 3) if tree == 0 else (TAPS[::-1], 4)
    m = np.zeros((n // 2, n))
    for k in range(n // 2):
        for j in range(8):
            m[k, (2 * k + j - offset) % n] += taps[j]
    return m


@functools.lru_cache(None)
def smooth_matrix(n, level):
    total = 0.0
    for tree in range(2):
        chain = np.eye(n)
        for step in range(level):
            chain = low_matrix(n >> step, tree) @ chain
        total = total + 0.5 * chain.T @ chain
    return total


def split_const(m):
    m = np.asarray(m, np.float32)
    hi = m.astype(BF16)
    lo = (m - hi.astype(np.float32)).astype(BF16)
    return hi, lo


@functools.lru_cache(None)
def constants(rows, cols):
    half = cols // 2
    n = 1024
    q = [smooth_matrix(n, level) for level in (1, 2, 3)]
    o = 256
    stack = lambda lo, hi: np.concatenate([m[o : o + 128, lo:hi] for m in q])
    send, recv = [], []
    for lo, hi, base in ((o - REACH, o, 0), (o + 128, o + 128 + REACH, 0)):
        u, s, vt = np.linalg.svd(stack(lo, hi), full_matrices=False)
        assert s[COEFS - 3] < 1e-14
        send.append(vt[:COEFS])
        recv.append(vt[:COEFS].T)
    below, above = send[0], send[1]
    own, edge = [], []
    for m in q:
        body = m[o : o + rows]
        own.append(body[:, o : o + rows])
        above_part = body[:REACH, o - REACH : o] @ recv[0]
        below_part = body[-REACH:, o + rows : o + rows + REACH] @ recv[1]
        nothing = np.zeros((REACH, COEFS))
        both = np.block([[above_part, nothing], [nothing, below_part]])
        hi, lo = split_const(both)
        edge.append(np.concatenate([hi, hi, lo], 1))
    c1, c2 = [], []
    for m in q:
        body = m[o : o + half]
        c1.append(body[:, o : o + half].T)
        left, right = body[:, o - REACH : o], body[:, o + half : o + half + REACH]
        nothing = np.zeros((half, COEFS))
        pad = np.zeros((half, 128 - 2 * COEFS - REACH))
        first = np.concatenate([left @ recv[0], nothing, right, pad], 1).T
        second = np.concatenate([nothing, right @ recv[1], left, pad], 1).T
        c2.append(np.stack([first, second]))
    qu = q[2] @ upsample_matrix(n)
    p = o // 4
    cu = np.concatenate(
        [
            qu[o : o + cols, p : p + cols // 4],
            qu[o : o + cols, p - RIM : p],
            qu[o : o + cols, p + cols // 4 : p + cols // 4 + RIM],
            np.zeros((cols, 128 - 2 * RIM)),
        ],
        1,
    ).T
    ru_own = split_const(qu[o : o + rows, p : p + rows // 4])
    above_part, below_part = qu[o : o + rows, p - RIM : p], qu[o : o + rows, p + rows // 4 : p + rows // 4 + RIM]
    assert not above_part[BAND_ROWS:].any() and not below_part[: rows - BAND_ROWS].any()
    nothing = np.zeros((BAND_ROWS, RIM))
    ru_rim = split_const(
        np.block([[above_part[:BAND_ROWS], nothing], [nothing, below_part[rows - BAND_ROWS :]]])
    )
    three = lambda pair: np.concatenate([pair[0], pair[0], pair[1]], 1)
    pair = lambda m: np.concatenate(split_const(m), 1)
    parts = dict(
        below=pair(below),
        above=pair(above),
        own=pair(np.concatenate(own)),
        ru_own=three(ru_own),
        ru_rim=three(ru_rim),
    )
    for level in range(LEVELS):
        parts[f"edge{level}"] = edge[level]
        parts[f"c1{level}hi"], parts[f"c1{level}lo"] = split_const(c1[level])
        for h in range(2):
            parts[f"c2{level}{h}hi"], parts[f"c2{level}{h}lo"] = split_const(c2[level][h])
    for h in range(2):
        parts[f"cu{h}hi"], parts[f"cu{h}lo"] = split_const(cu[:, h * half : (h + 1) * half])
    table, where, at = [], {}, 0
    for name, m in parts.items():
        high = -(-m.shape[0] // 16) * 16
        table.append(np.pad(np.asarray(m, np.float32), ((0, high - m.shape[0]), (0, half - m.shape[1]))))
        where[name] = (at, m.shape)
        at += high
    table = np.concatenate(table).astype(BF16)
    count = where["own"][0]
    return table, table[:count], where


class Table:
    def __init__(self, ref, where):
        self.ref, self.where = ref, where

    def __getitem__(self, name):
        at, (high, wide) = self.where[name]
        return self.ref[at : at + high, 0:wide]

    def pair(self, name):
        x = self[name]
        wide = x.shape[1] // 2
        return x[:, :wide], x[:, wide:]

    def two(self, name):
        return self[name + "hi"], self[name + "lo"]


def swap_pairs(count):
    return [(i, i ^ 1) for i in range(count)]


def odd_pairs(count):
    return [(i, (i - 1) % count if i % 2 == 0 else (i + 1) % count) for i in range(count)]


def column_steps(count):
    if count == 4:
        return [
            ([(i, i ^ k) for i in range(4)], k != 2, lambda c, k=k: c ^ k, lambda c, k=k: c ^ k)
            for k in (1, 3, 2)
        ]
    return [
        (
            [(i, (i + k) % count) for i in range(count)],
            k in (1, count - 1),
            lambda c, k=k: lax.rem(c + k, count),
            lambda c, k=k: lax.rem(c + count - k, count),
        )
        for k in [1, count - 1] + list(range(2, count - 1))
    ]


def split(x):
    hi = x.astype(BF16)
    return hi, (x - hi.astype(F32)).astype(BF16)


def dot(a, b, dims=((1,), (0,))):
    return lax.dot_general(a, b, (dims, ((), ())), preferred_element_type=F32)


def dot3(a, b, dims=((1,), (0,))):
    return dot(a[0], b[0], dims) + dot(a[1], b[0], dims) + dot(a[0], b[1], dims)


def lanes(shape):
    return lax.broadcasted_iota(jnp.int32, shape, 1)


def pack_chunk(out, ms_ref, to, count):
    bands, low = ms_ref.shape[0], ms_ref.shape[1]
    main = bands * low
    block = lambda k: pl.ds(pl.multiple_of(lax.rem(k + count, count) * 128, 128), 128)
    packed = None
    for i in range(bands):
        out[i * low : (i + 1) * low, :] = ms_ref[i, :, block(to)]
        left, right = ms_ref[i, :, block(to - 1)], ms_ref[i, :, block(to + 1)]
        rim = jnp.where(lanes(left.shape) >= 64, left, right)
        for g in range(low // RIM):
            slot = i * (low // RIM) + g
            rolled = pltpu.roll(rim[g * RIM : (g + 1) * RIM], (2 * RIM * slot + RIM) % 128, 1)
            packed = rolled if slot == 0 else jnp.where(lanes(rolled.shape) >= 2 * RIM * slot, rolled, packed)
    out[main : main + RIM, :] = packed


def pack_kernel(count, where, ms_ref, first_ref, last_ref, table_ref, *out_refs):
    c = lax.axis_index("col")
    table = Table(table_ref, where)
    main = ms_ref.shape[0] * ms_ref.shape[1]
    below, above = table.pair("below"), table.pair("above")
    for step, out in zip(column_steps(count), out_refs):
        to = step[2](c)
        pack_chunk(out, ms_ref, to, count)
        if step[1]:
            to_right = to == lax.rem(c + 1, count)
            edge = jnp.where(to_right, pltpu.roll(last_ref[...], REACH, 1), first_ref[...])
            v = tuple(jnp.where(to_right, x.astype(F32), y.astype(F32)).astype(BF16) for x, y in zip(below, above))
            out[main + RIM : main + RIM + COEFS, :] = dot3(v, split(edge[:, :REACH]), ((1,), (1,)))


def stage_kernel(count, where, ms_ref, pan_ref, table_ref, own_ref, top_ref, bot_ref):
    table = Table(table_ref, where)
    pack_chunk(own_ref, ms_ref, lax.axis_index("col"), count)
    rows = pan_ref.shape[0]
    for out, name, at in ((bot_ref, "below", rows - REACH), (top_ref, "above", 0)):
        full = dot3(table.pair(name), split(pan_ref[at : at + REACH, :]))
        for k in range(pan_ref.shape[1] // 128):
            out[k * COEFS : (k + 1) * COEFS, :] = full[:, k * 128 : (k + 1) * 128]


def rim_kernel(count, low, where, top_ref, bot_ref, table_ref, *refs):
    table = Table(table_ref, where)
    q = refs[:count]
    a_ref, b_ref, xh_ref = refs[count:]
    c, r = lax.axis_index("col"), lax.axis_index("row")
    steps = column_steps(count)
    bands = (q[0].shape[0] - RIM) // low
    main = bands * low
    even = lax.rem(r, 2) == 0
    first = q[1][main + RIM : main + RIM + COEFS, :]
    second = q[2][main + RIM : main + RIM + COEFS, :]
    first_is_right = steps[0][3](c) == lax.rem(c + 1, count)
    left = jnp.where(first_is_right, second, first)
    right = jnp.where(first_is_right, first, second)
    filler = jnp.zeros((128 - 2 * COEFS, 128), F32)
    xh = jnp.concatenate([left, right, filler], 0).T
    xh_ref[...] = xh
    height = top_ref.shape[0]
    per = low // RIM
    total = count * bands

    def fill(out, bottom):
        out[0:height, :] = (bot_ref if bottom else top_ref)[...]
        v = table.pair("below" if bottom else "above")
        edge = xh[xh.shape[0] - REACH :] if bottom else xh[:REACH]
        out[height : height + COEFS, :] = dot3(v, split(edge))
        base = height + COEFS
        packed = None
        for n in range(total):
            ref, i = q[n // bands], n % bands
            row = (i + 1) * low - RIM if bottom else i * low
            out[base + n * RIM : base + (n + 1) * RIM, :] = ref[row : row + RIM, :]
            slot = per * (i + 1) - 1 if bottom else per * i
            rim = pltpu.roll(ref[main : main + RIM, :], (2 * RIM * (n % 4 - slot)) % 128, 1)
            packed = rim if n % 4 == 0 else jnp.where(lanes(rim.shape) >= 2 * RIM * (n % 4), rim, packed)
            if n % 4 == 3 or n == total - 1:
                spot = base + total * RIM + (n // 4) * RIM
                out[spot : spot + RIM, :] = packed

    @pl.when(even)
    def _():
        fill(a_ref, 1)
        fill(b_ref, 0)

    @pl.when(jnp.logical_not(even))
    def _():
        fill(a_ref, 0)
        fill(b_ref, 1)


def own_rims(own_right, own_left, xh):
    inner = lanes(xh.shape) < 2 * COEFS
    return (
        jnp.where(inner, xh, pltpu.roll(own_right, 2 * COEFS, 1)),
        jnp.where(inner, xh, pltpu.roll(own_left, 2 * COEFS + REACH, 1)),
    )


def columns(t, cols, table, level):
    half = cols // 2
    out = []
    for h in range(2):
        own = tuple(x[:, h * half : (h + 1) * half] for x in t)
        rim = tuple(x[:, cols + h * 128 : cols + (h + 1) * 128] for x in t)
        out.append(
            dot3(own, table.two(f"c1{level}")) + dot3(rim, table.two(f"c2{level}{h}"))
        )
    return out


def low_columns(x, table):
    return jnp.concatenate([dot3(x, table.two(f"cu{h}")) for h in range(2)], 1)


def local_kernel(count, low, where, gains_ref, *refs):
    q, refs = refs[:count], refs[count:]
    pan_ref, xh_ref, table_ref, part_ref, xe, e3, mext = refs
    table = Table(table_ref, where)
    c = lax.axis_index("col")
    steps = column_steps(count)
    bands = (q[0].shape[0] - RIM) // low
    main = bands * low
    rows, cols = pan_ref.shape
    half = cols // 2
    xe[:, 0:cols] = pan_ref[...]
    f, s = own_rims(pan_ref[:, half : half + 128], pan_ref[:, half - 128 : half], xh_ref[...])
    xe[:, cols : cols + 128] = f
    xe[:, cols + 128 : cols + 256] = s
    x = split(xe[...])
    for level in range(LEVELS):
        rs = slice(level * rows, (level + 1) * rows)
        t = split(dot3(tuple(m[rs] for m in table.pair("own")), x))
        for h, e in enumerate(columns(t, cols, table, level)):
            e3[level, :, h * half : (h + 1) * half] = e
    per = low // RIM
    for n in range(count * bands):
        ref, i = q[n // bands], n % bands
        mext[n * low : (n + 1) * low, 0:128] = ref[i * low : (i + 1) * low, :]
        for g in range(per):
            at = n * low + g * RIM
            mext[at : at + RIM, 128:256] = pltpu.roll(
                ref[main : main + RIM, :], (-2 * RIM * (i * per + g)) % 128, 1
            )
    for j in range(count):
        src = c if j == 0 else steps[j - 1][3](c)
        y = low_columns(split(mext[j * main : (j + 1) * main, :]), table)
        for i in range(bands):
            band = src * bands + i
            hi, lo = split(y[i * low : (i + 1) * low])
            g1, g2, g3 = gains_ref[band, 0], gains_ref[band, 1], gains_ref[band, 2]
            part_ref[j * bands + i] = (
                dot(table["ru_own"], jnp.concatenate([hi, lo, hi], 0))
                + g1 * pan_ref[...]
                + (g2 - g1) * e3[0]
                + (g3 - g2) * e3[1]
                - g3 * e3[2]
            )


def main_kernel(count, low, bands, where, gains_ref, *refs):
    part_ref, a_ref, b_ref, table_ref, out_ref, xe, de, mext, obuf, sems = refs
    table = Table(table_ref, where)
    c, r = lax.axis_index("col"), lax.axis_index("row")
    steps = column_steps(count)
    even = lax.rem(r, 2) == 0
    total, rows, cols = part_ref.shape
    half = cols // 2
    blocks = cols // 128
    mid = half // 128
    base = (blocks + 1) * COEFS
    for ref, below in ((a_ref, even), (b_ref, jnp.logical_not(even))):
        at = pl.ds(pl.multiple_of(jnp.where(below, COEFS, 0), 8), COEFS)
        piece = lambda k: ref[k * COEFS : (k + 1) * COEFS, :]
        for k in range(blocks):
            xe[at, k * 128 : (k + 1) * 128] = piece(k)
        f, s = own_rims(piece(mid), piece(mid - 1), piece(blocks))
        xe[at, cols : cols + 128] = f
        xe[at, cols + 128 : cols + 256] = s
        for n in range(total):
            at = pl.ds(pl.multiple_of(n * 2 * RIM + jnp.where(below, RIM, 0), 16), RIM)
            mext[at, 0:128] = ref[base + n * RIM : base + (n + 1) * RIM, :]
            spot = base + total * RIM + (n // 4) * RIM
            mext[at, 128:256] = pltpu.roll(ref[spot : spot + RIM, :], (-2 * RIM * (n % 4)) % 128, 1)
    x = split(xe[...])
    for level in range(LEVELS):
        for h, z in enumerate(columns(x, cols, table, level)):
            hi, lo = split(z)
            de[level, :, h * half : (h + 1) * half] = dot(table[f"edge{level}"], jnp.concatenate([hi, lo, hi], 0))
    copies = []
    for j in range(count):
        src = c if j == 0 else steps[j - 1][3](c)
        high = bands * 2 * RIM
        y = low_columns(split(mext[j * high : (j + 1) * high, :]), table)
        for i in range(bands):
            band = src * bands + i
            n = j * bands + i
            hi, lo = split(y[i * 2 * RIM : (i + 1) * 2 * RIM])
            g1, g2, g3 = gains_ref[band, 0], gains_ref[band, 1], gains_ref[band, 2]
            add = dot(table["ru_rim"], jnp.concatenate([hi, lo, hi], 0))
            fix = (g2 - g1) * de[0] + (g3 - g2) * de[1] - g3 * de[2]
            top = add[:BAND_ROWS]
            top = jnp.concatenate([top[:REACH] + fix[:REACH], top[REACH:]], 0)
            low_end = add[BAND_ROWS:]
            low_end = jnp.concatenate(
                [low_end[: BAND_ROWS - REACH], low_end[BAND_ROWS - REACH :] + fix[REACH:]], 0
            )
            obuf[n, 0:BAND_ROWS] = part_ref[n, 0:BAND_ROWS] + top
            obuf[n, BAND_ROWS : rows - BAND_ROWS] = part_ref[n, BAND_ROWS : rows - BAND_ROWS]
            obuf[n, rows - BAND_ROWS :] = part_ref[n, rows - BAND_ROWS :] + low_end
            copy = pltpu.make_async_copy(obuf.at[n], out_ref.at[band], sems.at[n])
            copy.start()
            copies.append(copy)
    for copy in copies:
        copy.wait()


def on_device(multispectral, panchromatic, band_gains):
    count, row_count = lax.axis_size("col"), lax.axis_size("row")
    bands, low, _ = multispectral.shape
    rows, cols = panchromatic.shape
    total = count * bands
    table, small, where = constants(rows, cols)
    steps = column_steps(count)
    chunk = bands * low + RIM
    shape = lambda n, m=128: jax.ShapeDtypeStruct((n, m), F32)
    whole = pl.BlockSpec(memory_space=VMEM)
    heights = [chunk + (COEFS if step[1] else 0) for step in steps]
    last = cols // 128 - 1
    packed = pl.pallas_call(
        functools.partial(pack_kernel, count, where),
        out_shape=[shape(h) for h in heights],
        grid=(1,),
        in_specs=[
            pl.BlockSpec(multispectral.shape, lambda i: (0, 0, 0)),
            pl.BlockSpec((rows, 128), lambda i: (0, 0)),
            pl.BlockSpec((rows, 128), lambda i: (0, last)),
            pl.BlockSpec(small.shape, lambda i: (0, 0)),
        ],
        out_specs=[pl.BlockSpec((h, 128), lambda i: (0, 0)) for h in heights],
        name="pack",
    )(multispectral, panchromatic, panchromatic, jnp.asarray(small))
    params = lambda mib: pltpu.CompilerParams(vmem_limit_bytes=mib << 20)
    cost = lambda flops: pl.CostEstimate(flops=flops, bytes_accessed=10**6, transcendentals=0)
    table = jnp.asarray(table)
    height = cols // 128 * COEFS
    own, top, bot = pl.pallas_call(
        functools.partial(stage_kernel, count, where),
        out_shape=[shape(chunk), shape(height), shape(height)],
        in_specs=[whole] * 3,
        out_specs=[whole] * 3,
        compiler_params=params(8),
        cost_estimate=cost(10**9),
        name="stage",
    )(multispectral, panchromatic, table)
    q = [own] + [lax.ppermute(x, "col", step[0]) for x, step in zip(packed, steps)]
    sent = height + COEFS + total * RIM + -(-total // 4) * RIM
    a, b, xh = pl.pallas_call(
        functools.partial(rim_kernel, count, low, where),
        out_shape=[shape(sent), shape(sent), shape(rows)],
        in_specs=[whole] * (3 + count),
        out_specs=[whole] * 3,
        compiler_params=params(8),
        name="rim",
    )(top, bot, table, *q)
    a = lax.ppermute(a, "row", swap_pairs(row_count))
    b = lax.ppermute(b, "row", odd_pairs(row_count))
    smem = pl.BlockSpec(memory_space=pltpu.SMEM)
    part = pl.pallas_call(
        functools.partial(local_kernel, count, low, where),
        out_shape=jax.ShapeDtypeStruct((total, rows, cols), F32),
        in_specs=[smem] + [whole] * (count + 3),
        out_specs=whole,
        scratch_shapes=[
            VMEM((rows, cols + 256), F32),
            VMEM((LEVELS, rows, cols), F32),
            VMEM((total * low, 256), F32),
        ],
        compiler_params=params(16),
        cost_estimate=cost(4 * 10**9),
        name="local",
    )(band_gains, *q, panchromatic, xh, table)
    return pl.pallas_call(
        functools.partial(main_kernel, count, low, bands, where),
        out_shape=jax.ShapeDtypeStruct((total, rows, cols), F32),
        in_specs=[smem] + [whole] * 4,
        out_specs=pl.BlockSpec(memory_space=pltpu.HBM),
        scratch_shapes=[
            VMEM((2 * COEFS, cols + 256), F32),
            VMEM((LEVELS, 2 * REACH, cols), F32),
            VMEM((total * 2 * RIM, 256), F32),
            VMEM((total, rows, cols), F32),
            pltpu.SemaphoreType.DMA((total,)),
        ],
        compiler_params=params(16),
        name="combine",
    )(band_gains, part, a, b, table)


def solution(mesh):
    in_specs = (P("col", "row", None), P("row", "col"), P())
    out_specs = P(None, "row", "col")
    return jax.shard_map(
        on_device, mesh=mesh, in_specs=in_specs, out_specs=out_specs, check_vma=False
    )
```

```python
import functools

import jax
import jax.numpy as jnp
import numpy as np
from jax import lax
from jax.experimental import pallas as pl
from jax.experimental.pallas import tpu as pltpu
from jax.sharding import PartitionSpec as P

LEVELS = 3
TAPS = [
    0.2303778133088964,
    0.7148465705529155,
    0.6308807679298587,
    -0.0279837694168599,
    -0.1870348117190931,
    0.0308413818355607,
    0.0328830116668852,
    -0.010597401785069,
]
REACH = 48
COEFS = 24
RIM = 16
BAND_ROWS = 56
VMEM = pltpu.VMEM
F32, BF16 = jnp.float32, jnp.bfloat16


def keys_weight(t):
    t = abs(t)
    if t <= 1.0:
        return 1.5 * t**3 - 2.5 * t**2 + 1.0
    return -0.5 * t**3 + 2.5 * t**2 - 4.0 * t + 2.0 if t < 2.0 else 0.0


def upsample_matrix(n):
    m = np.zeros((n, n // 4))
    for y in range(n):
        centre = (y + 0.5) / 4.0 - 0.5
        for k in range(int(np.floor(centre)) - 1, int(np.floor(centre)) + 3):
            m[y, k % (n // 4)] += keys_weight(centre - k)
    return m


def low_matrix(n, tree):
    taps, offset = (TAPS, 3) if tree == 0 else (TAPS[::-1], 4)
    m = np.zeros((n // 2, n))
    for k in range(n // 2):
        for j in range(8):
            m[k, (2 * k + j - offset) % n] += taps[j]
    return m


@functools.lru_cache(None)
def smooth_matrix(n, level):
    total = 0.0
    for tree in range(2):
        chain = np.eye(n)
        for step in range(level):
            chain = low_matrix(n >> step, tree) @ chain
        total = total + 0.5 * chain.T @ chain
    return total


def split_const(m):
    m = np.asarray(m, np.float32)
    hi = m.astype(BF16)
    lo = (m - hi.astype(np.float32)).astype(BF16)
    return hi, lo


@functools.lru_cache(None)
def constants(rows, cols):
    half = cols // 2
    n = 1024
    q = [smooth_matrix(n, level) for level in (1, 2, 3)]
    o = 256
    stack = lambda lo, hi: np.concatenate([m[o : o + 128, lo:hi] for m in q])
    send, recv = [], []
    for lo, hi, base in ((o - REACH, o, 0), (o + 128, o + 128 + REACH, 0)):
        u, s, vt = np.linalg.svd(stack(lo, hi), full_matrices=False)
        assert s[COEFS - 3] < 1e-14
        send.append(vt[:COEFS])
        recv.append(vt[:COEFS].T)
    below, above = send[0], send[1]
    own, edge = [], ([], [])
    for m in q:
        body = m[o : o + rows]
        own.append(body[:, o : o + rows])
        edge[0].append(body[:REACH, o - REACH : o] @ recv[0])
        edge[1].append(body[-REACH:, o + rows : o + rows + REACH] @ recv[1])
    c1, c2 = [], []
    for m in q:
        body = m[o : o + half]
        c1.append(body[:, o : o + half].T)
        left, right = body[:, o - REACH : o], body[:, o + half : o + half + REACH]
        nothing = np.zeros((half, COEFS))
        first = np.concatenate([left @ recv[0], nothing, right], 1).T
        second = np.concatenate([nothing, right @ recv[1], left], 1).T
        c2.append((first, second))
    qu = q[2] @ upsample_matrix(n)
    p = o // 4
    low = rows // 4
    cu = np.concatenate(
        [
            qu[o : o + cols, p : p + cols // 4],
            qu[o : o + cols, p - RIM : p],
            qu[o : o + cols, p + cols // 4 : p + cols // 4 + RIM],
        ],
        1,
    ).T
    ru = qu[o : o + rows]
    ru_own, ru_rims = ru[:, p : p + low], (ru[:, p - RIM : p], ru[:, p + low : p + low + RIM])
    ru_ends = (ru_rims[0][:BAND_ROWS], ru_rims[1][rows - BAND_ROWS :])
    assert not ru_rims[0][BAND_ROWS:].any() and not ru_rims[1][: rows - BAND_ROWS].any()

    def three(m):
        hi, lo = split_const(m)
        return np.concatenate([hi, hi, lo], 1)

    pair = lambda m: np.concatenate(split_const(m), 1)
    parts = dict(below=pair(below), above=pair(above))
    for side in range(2):
        parts[f"edge{side}"] = np.concatenate([three(m) for m in edge[side]])
    for side in range(2):
        parts[f"ru{side}"] = three(np.concatenate([ru_own, ru_rims[side]], 1))
    for side in range(2):
        parts[f"end{side}"] = three(ru_ends[side])
    for level in range(LEVELS):
        parts[f"own{level}"] = pair(own[level])
        parts[f"c1{level}hi"], parts[f"c1{level}lo"] = split_const(c1[level])
        for h in range(2):
            parts[f"c2{level}{h}hi"], parts[f"c2{level}{h}lo"] = split_const(c2[level][h])
    for h in range(2):
        parts[f"cu{h}hi"], parts[f"cu{h}lo"] = split_const(cu[:, h * half : (h + 1) * half])
    table, where, at = [], {}, 0
    for name, m in parts.items():
        high = -(-m.shape[0] // 16) * 16
        table.append(np.pad(np.asarray(m, np.float32), ((0, high - m.shape[0]), (0, half - m.shape[1]))))
        where[name] = (at, m.shape)
        at += high
    table = np.concatenate(table).astype(BF16)
    return table, table[: where["edge0"][0]], where


class Table:
    def __init__(self, ref, where):
        self.ref, self.where = ref, where

    def __getitem__(self, name):
        at, (high, wide) = self.where[name]
        return self.ref[at : at + high, 0:wide]

    def pair(self, name):
        x = self[name]
        wide = x.shape[1] // 2
        return x[:, :wide], x[:, wide:]

    def side(self, name, below):
        (first, (high, wide)), (second, _) = self.where[name + "0"], self.where[name + "1"]
        at = pl.multiple_of(jnp.where(below, second, first), 16)
        return self.ref[pl.ds(at, high), 0:wide]

    def two(self, name):
        return self[name + "hi"], self[name + "lo"]


def swap_pairs(count):
    return [(i, i ^ 1) for i in range(count)]


def odd_pairs(count):
    return [(i, (i - 1) % count if i % 2 == 0 else (i + 1) % count) for i in range(count)]


def column_steps(count):
    if count == 4:
        return [
            ([(i, i ^ k) for i in range(4)], k != 2, lambda c, k=k: c ^ k, lambda c, k=k: c ^ k)
            for k in (1, 3, 2)
        ]
    return [
        (
            [(i, (i + k) % count) for i in range(count)],
            k in (1, count - 1),
            lambda c, k=k: lax.rem(c + k, count),
            lambda c, k=k: lax.rem(c + count - k, count),
        )
        for k in [1, count - 1] + list(range(2, count - 1))
    ]


def split(x):
    hi = x.astype(BF16)
    return hi, (x - hi.astype(F32)).astype(BF16)


def dot(a, b, dims=((1,), (0,))):
    return lax.dot_general(a, b, (dims, ((), ())), preferred_element_type=F32)


def dot3(a, b, dims=((1,), (0,))):
    return dot(a[0], b[0], dims) + dot(a[1], b[0], dims) + dot(a[0], b[1], dims)


def rows3(a, b):
    high = a[0].shape[0]
    both = dot(jnp.concatenate(a, 0), b[0])
    return both[:high] + both[high:] + dot(a[0], b[1])


def three_high(x):
    if x.shape[0] % 16:
        hi = x.astype(BF16).astype(F32)
        return jnp.concatenate([hi, x - hi, hi], 0).astype(BF16)
    hi, lo = split(x)
    return jnp.concatenate([hi, lo, hi], 0)


def lanes(shape):
    return lax.broadcasted_iota(jnp.int32, shape, 1)


def pack_chunk(out, ms_ref, to, count):
    bands, low = ms_ref.shape[0], ms_ref.shape[1]
    main = bands * low
    block = lambda k: pl.ds(pl.multiple_of(lax.rem(k + count, count) * 128, 128), 128)
    packed = None
    for i in range(bands):
        out[i * low : (i + 1) * low, :] = ms_ref[i, :, block(to)]
        left, right = ms_ref[i, :, block(to - 1)], ms_ref[i, :, block(to + 1)]
        rim = jnp.where(lanes(left.shape) >= 64, left, right)
        for g in range(low // RIM):
            slot = i * (low // RIM) + g
            rolled = pltpu.roll(rim[g * RIM : (g + 1) * RIM], (2 * RIM * slot + RIM) % 128, 1)
            packed = rolled if slot == 0 else jnp.where(lanes(rolled.shape) >= 2 * RIM * slot, rolled, packed)
    out[main : main + RIM, :] = packed


def pack_kernel(count, where, ms_ref, first_ref, last_ref, table_ref, *out_refs):
    c = lax.axis_index("col")
    table = Table(table_ref, where)
    main = ms_ref.shape[0] * ms_ref.shape[1]
    below, above = table.pair("below"), table.pair("above")
    for step, out in zip(column_steps(count), out_refs):
        to = step[2](c)
        pack_chunk(out, ms_ref, to, count)
        if step[1]:
            to_right = to == lax.rem(c + 1, count)
            edge = jnp.where(to_right, pltpu.roll(last_ref[...], REACH, 1), first_ref[...])
            v = tuple(jnp.where(to_right, x.astype(F32), y.astype(F32)).astype(BF16) for x, y in zip(below, above))
            out[main + RIM : main + RIM + COEFS, :] = dot3(v, split(edge[:, :REACH]), ((1,), (1,)))


def stage_kernel(count, where, first, *refs):
    ms_hbm, pan_hbm, table_hbm, own_ref, top_ref, bot_ref, pan_ref, table_ref, ms_ref, sems = refs
    rest = table_ref.shape[0] - first
    moves = [
        (table_hbm.at[pl.ds(0, first)], table_ref.at[pl.ds(0, first)]),
        (pan_hbm, pan_ref),
        (ms_hbm, ms_ref),
        (table_hbm.at[pl.ds(first, rest)], table_ref.at[pl.ds(first, rest)]),
    ]
    copies = [pltpu.make_async_copy(x, y, sems.at[k]) for k, (x, y) in enumerate(moves)]
    for copy in copies:
        copy.start()
    for copy in copies[:3]:
        copy.wait()
    table = Table(table_ref, where)
    pack_chunk(own_ref, ms_ref, lax.axis_index("col"), count)
    rows = pan_ref.shape[0]
    for out, name, at in ((bot_ref, "below", rows - REACH), (top_ref, "above", 0)):
        full = dot3(table.pair(name), split(pan_ref[at : at + REACH, :]))
        for k in range(pan_ref.shape[1] // 128):
            out[k * COEFS : (k + 1) * COEFS, :] = full[:, k * 128 : (k + 1) * 128]
    copies[3].wait()


def rim_kernel(count, low, where, top_ref, bot_ref, table_ref, *refs):
    table = Table(table_ref, where)
    q = refs[:count]
    a_ref, b_ref, xh_ref = refs[count:]
    c, r = lax.axis_index("col"), lax.axis_index("row")
    steps = column_steps(count)
    bands = (q[0].shape[0] - RIM) // low
    main = bands * low
    even = lax.rem(r, 2) == 0
    first = q[1][main + RIM : main + RIM + COEFS, :]
    second = q[2][main + RIM : main + RIM + COEFS, :]
    first_is_right = steps[0][3](c) == lax.rem(c + 1, count)
    left = jnp.where(first_is_right, second, first)
    right = jnp.where(first_is_right, first, second)
    filler = jnp.zeros((128 - 2 * COEFS, 128), F32)
    xh = jnp.concatenate([left, right, filler], 0).T
    xh_ref[...] = xh
    height = top_ref.shape[0]
    per = low // RIM
    total = count * bands

    def fill(out, bottom):
        out[0:height, :] = (bot_ref if bottom else top_ref)[...]
        v = table.pair("below" if bottom else "above")
        edge = xh[xh.shape[0] - REACH :] if bottom else xh[:REACH]
        out[height : height + COEFS, :] = dot3(v, split(edge))
        base = height + COEFS
        packed = None
        for n in range(total):
            ref, i = q[n // bands], n % bands
            row = (i + 1) * low - RIM if bottom else i * low
            out[base + n * RIM : base + (n + 1) * RIM, :] = ref[row : row + RIM, :]
            slot = per * (i + 1) - 1 if bottom else per * i
            rim = pltpu.roll(ref[main : main + RIM, :], (2 * RIM * (n % 4 - slot)) % 128, 1)
            packed = rim if n % 4 == 0 else jnp.where(lanes(rim.shape) >= 2 * RIM * (n % 4), rim, packed)
            if n % 4 == 3 or n == total - 1:
                spot = base + total * RIM + (n // 4) * RIM
                out[spot : spot + RIM, :] = packed

    @pl.when(even)
    def _():
        fill(a_ref, 1)
        fill(b_ref, 0)

    @pl.when(jnp.logical_not(even))
    def _():
        fill(a_ref, 0)
        fill(b_ref, 1)


def own_rims(own_right, own_left, xh):
    inner = lanes(xh.shape) < 2 * COEFS
    return (
        jnp.where(inner, xh, pltpu.roll(own_right, 2 * COEFS, 1)),
        jnp.where(inner, xh, pltpu.roll(own_left, 2 * COEFS + REACH, 1)),
    )


def columns(x, cols, table, level):
    half = cols // 2
    high = x.shape[0]
    wide = 2 * COEFS + REACH
    main = rows3(split(jnp.concatenate([x[:, :half], x[:, half:cols]], 0)), table.two(f"c1{level}"))
    out = []
    for h in range(2):
        rim = split(x[:, cols + h * 128 : cols + h * 128 + wide])
        product = dot3 if high % 16 else rows3
        out.append(main[h * high : (h + 1) * high] + product(rim, table.two(f"c2{level}{h}")))
    return out


def low_columns(x_ref, y_ref, table):
    x = split(x_ref[:, 0 : 128 + 2 * RIM])
    half = y_ref.shape[1] // 2
    for h in range(2):
        y_ref[:, h * half : (h + 1) * half] = rows3(x, table.two(f"cu{h}"))


def fill_rows(xe, at, cols, piece, xh):
    blocks = cols // 128
    for k in range(blocks):
        xe[at, k * 128 : (k + 1) * 128] = piece(k)
    f, s = own_rims(piece(blocks // 2), piece(blocks // 2 - 1), xh)
    xe[at, cols : cols + 128] = f
    xe[at, cols + 128 : cols + 256] = s


def coef_piece(ref):
    return lambda k: ref[k * COEFS : (k + 1) * COEFS, :]


def band_rims(mext, ref, total, base, high, skip):
    for n in range(total):
        at = slice(n * high + skip, n * high + skip + RIM)
        mext[at, 0:128] = ref[base + n * RIM : base + (n + 1) * RIM, :]
        spot = base + total * RIM + (n // 4) * RIM
        mext[at, 128:256] = pltpu.roll(ref[spot : spot + RIM, :], (-2 * RIM * (n % 4)) % 128, 1)


def local_kernel(count, low, where, gains_ref, *refs):
    q, refs = refs[:count], refs[count:]
    pan_ref, xh_ref, a_ref, table_ref, part_ref, gains_out, xe, tr, e3, mext, y_ref = refs
    table = Table(table_ref, where)
    c, r = lax.axis_index("col"), lax.axis_index("row")
    below = lax.rem(r, 2) == 0
    steps = column_steps(count)
    bands = (q[0].shape[0] - RIM) // low
    total = count * bands
    main = bands * low
    rows, cols = pan_ref.shape
    half = cols // 2
    per = low // RIM
    high = low + RIM
    for n in range(total):
        ref, i = q[n // bands], n % bands
        mext[n * high : n * high + low, 0:128] = ref[i * low : (i + 1) * low, :]
        for g in range(per):
            at = n * high + g * RIM
            mext[at : at + RIM, 128:256] = pltpu.roll(
                ref[main : main + RIM, :], (-2 * RIM * (i * per + g)) % 128, 1
            )
    band_rims(mext, a_ref, total, (cols // 128 + 1) * COEFS, high, low)
    low_columns(mext, y_ref, table)
    fill_rows(xe, slice(0, rows), cols, lambda k: pan_ref[:, k * 128 : (k + 1) * 128], xh_ref[...])
    fill_rows(xe, slice(rows, rows + COEFS), cols, coef_piece(a_ref), a_ref[cols // 128 * COEFS : (cols // 128 + 1) * COEFS, :])
    hi, lo = split(xe[0:rows, :])
    both = jnp.concatenate([hi, lo], 0)
    added = dot(table.side("edge", below), three_high(xe[rows : rows + COEFS, :]))
    for level in range(LEVELS):
        ohi, olo = table.pair(f"own{level}")
        tr[level] = dot(jnp.concatenate([ohi, ohi], 1), both) + dot(olo, hi)
        at = pl.ds(pl.multiple_of(jnp.where(below, rows - REACH, 0), 16), REACH)
        tr[level, at, :] = tr[level, at, :] + added[level * REACH : (level + 1) * REACH]
        for h, e in enumerate(columns(tr[level], cols, table, level)):
            e3[level, :, h * half : (h + 1) * half] = e
    for j in range(count):
        src = c if j == 0 else steps[j - 1][3](c)
        for i in range(bands):
            n = j * bands + i
            band = src * bands + i
            g1, g2, g3 = gains_ref[band, 0], gains_ref[band, 1], gains_ref[band, 2]
            for k, g in enumerate((g2 - g1, g3 - g2, -g3)):
                gains_out[3 * n + k : 3 * n + k + 1, :] = jnp.full((1, cols), g, F32)
            part_ref[n] = (
                dot(table.side("ru", below), three_high(y_ref[n * high : (n + 1) * high, :]))
                + g1 * pan_ref[...]
                + (g2 - g1) * e3[0]
                + (g3 - g2) * e3[1]
                - g3 * e3[2]
            )


def main_kernel(count, low, bands, where, *refs):
    part_ref, gains_ref, b_ref, table_ref, out_ref, xe, de, mext, y_ref, obuf, sems = refs
    table = Table(table_ref, where)
    c, r = lax.axis_index("col"), lax.axis_index("row")
    steps = column_steps(count)
    below = lax.rem(r, 2) == 1
    total, rows, cols = part_ref.shape
    half = cols // 2
    blocks = cols // 128
    source = [c if j == 0 else steps[j - 1][3](c) for j in range(count)]
    band = [source[n // bands] * bands + n % bands for n in range(total)]
    done = pl.ds(pl.multiple_of(jnp.where(below, 0, BAND_ROWS), 8), rows - BAND_ROWS)
    late = pl.ds(pl.multiple_of(jnp.where(below, rows - BAND_ROWS, 0), 8), BAND_ROWS)
    copies = [
        pltpu.make_async_copy(part_ref.at[n, done], out_ref.at[band[n], done], sems.at[0, n])
        for n in range(total)
    ]
    for copy in copies:
        copy.start()
    band_rims(mext, b_ref, total, (blocks + 1) * COEFS, RIM, 0)
    low_columns(mext, y_ref, table)
    fill_rows(xe, slice(0, COEFS), cols, coef_piece(b_ref), b_ref[blocks * COEFS : (blocks + 1) * COEFS, :])
    edges = table.side("edge", below)
    gap = BAND_ROWS - REACH
    de[:, pl.ds(pl.multiple_of(jnp.where(below, 0, REACH), 8), gap), :] = jnp.zeros((LEVELS, gap, cols), F32)
    at = pl.ds(pl.multiple_of(jnp.where(below, gap, 0), 8), REACH)
    for level in range(LEVELS):
        for h, z in enumerate(columns(xe[...], cols, table, level)):
            de[level, at, h * half : (h + 1) * half] = dot(edges[level * REACH : (level + 1) * REACH], three_high(z))
    for n in range(total):
        g = [gains_ref[3 * n + k : 3 * n + k + 1, :] for k in range(LEVELS)]
        obuf[n] = (
            part_ref[n, late, :]
            + dot(table.side("end", below), three_high(y_ref[n * RIM : (n + 1) * RIM, :]))
            + g[0] * de[0]
            + g[1] * de[1]
            + g[2] * de[2]
        )
        copy = pltpu.make_async_copy(obuf.at[n], out_ref.at[band[n], late], sems.at[1, n])
        copy.start()
        copies.append(copy)
    for copy in copies:
        copy.wait()


def on_device(multispectral, panchromatic, band_gains):
    count, row_count = lax.axis_size("col"), lax.axis_size("row")
    bands, low, _ = multispectral.shape
    rows, cols = panchromatic.shape
    total = count * bands
    table, small, where = constants(rows, cols)
    steps = column_steps(count)
    chunk = bands * low + RIM
    shape = lambda n, m=128: jax.ShapeDtypeStruct((n, m), F32)
    whole = pl.BlockSpec(memory_space=VMEM)
    heights = [chunk + (COEFS if step[1] else 0) for step in steps]
    last = cols // 128 - 1
    packed = pl.pallas_call(
        functools.partial(pack_kernel, count, where),
        out_shape=[pltpu.VMEM((h, 128), F32) for h in heights],
        grid=(1,),
        in_specs=[
            pl.BlockSpec(multispectral.shape, lambda i: (0, 0, 0)),
            pl.BlockSpec((rows, 128), lambda i: (0, 0)),
            pl.BlockSpec((rows, 128), lambda i: (0, last)),
            pl.BlockSpec(small.shape, lambda i: (0, 0)),
        ],
        out_specs=[whole for h in heights],
        name="pack",
    )(*(pltpu.with_memory_space_constraint(x, pltpu.HBM) for x in (multispectral, panchromatic, panchromatic, jnp.asarray(small))))
    params = lambda mib: pltpu.CompilerParams(vmem_limit_bytes=mib << 20)
    cost = lambda flops: pl.CostEstimate(flops=flops, bytes_accessed=10**6, transcendentals=0)
    table = jnp.asarray(table)
    height = cols // 128 * COEFS
    first = small.shape[0]
    in_hbm = lambda *xs: [pltpu.with_memory_space_constraint(x, pltpu.HBM) for x in xs]
    own, top, bot, pan, table = pl.pallas_call(
        functools.partial(stage_kernel, count, where, first),
        out_shape=[
            VMEM((chunk, 128), F32),
            VMEM((height, 128), F32),
            VMEM((height, 128), F32),
            VMEM((rows, cols), F32),
            VMEM(table.shape, BF16),
        ],
        in_specs=[pl.BlockSpec(memory_space=pltpu.HBM)] * 3,
        out_specs=[whole] * 5,
        scratch_shapes=[VMEM(multispectral.shape, F32), pltpu.SemaphoreType.DMA((4,))],
        compiler_params=params(8),
        cost_estimate=cost(10**9),
        name="stage",
    )(*in_hbm(multispectral, panchromatic, table))
    q = [own] + [lax.ppermute(x, "col", step[0]) for x, step in zip(packed, steps)]
    sent = height + COEFS + total * RIM + -(-total // 4) * RIM
    a, b, xh = pl.pallas_call(
        functools.partial(rim_kernel, count, low, where),
        out_shape=[shape(sent), shape(sent), shape(rows)],
        in_specs=[whole] * (3 + count),
        out_specs=[whole] * 3,
        compiler_params=params(8),
        name="rim",
    )(top, bot, table, *q)
    a = lax.ppermute(a, "row", swap_pairs(row_count))
    b = lax.ppermute(b, "row", odd_pairs(row_count))
    smem = pl.BlockSpec(memory_space=pltpu.SMEM)
    part, scaled = pl.pallas_call(
        functools.partial(local_kernel, count, low, where),
        out_shape=[jax.ShapeDtypeStruct((total, rows, cols), F32), shape(LEVELS * total, cols)],
        in_specs=[smem] + [whole] * (count + 4),
        out_specs=[whole] * 2,
        scratch_shapes=[
            VMEM((rows + COEFS, cols + 256), F32),
            VMEM((LEVELS, rows, cols + 256), F32),
            VMEM((LEVELS, rows, cols), F32),
            VMEM((total * (low + RIM), 256), F32),
            VMEM((total * (low + RIM), cols), F32),
        ],
        compiler_params=params(16),
        cost_estimate=cost(4 * 10**9),
        name="local",
    )(band_gains, *q, pan, xh, a, table)
    return pl.pallas_call(
        functools.partial(main_kernel, count, low, bands, where),
        out_shape=jax.ShapeDtypeStruct((total, rows, cols), F32),
        in_specs=[whole] * 4,
        out_specs=pl.BlockSpec(memory_space=pltpu.HBM),
        scratch_shapes=[
            VMEM((COEFS, cols + 256), F32),
            VMEM((LEVELS, BAND_ROWS, cols), F32),
            VMEM((total * RIM, 256), F32),
            VMEM((total * RIM, cols), F32),
            VMEM((total, BAND_ROWS, cols), F32),
            pltpu.SemaphoreType.DMA((2, total)),
        ],
        compiler_params=params(16),
        name="combine",
    )(part, scaled, b, table)


def solution(mesh):
    in_specs = (P("col", "row", None), P("row", "col"), P())
    out_specs = P(None, "row", "col")
    return jax.shard_map(
        on_device, mesh=mesh, in_specs=in_specs, out_specs=out_specs, check_vma=False
    )
```

```python
import functools

import jax
import jax.numpy as jnp
import numpy as np
from jax import lax
from jax.experimental import pallas as pl
from jax.experimental.pallas import tpu as pltpu
from jax.sharding import PartitionSpec as P

LEVELS = 3
TAPS = [
    0.2303778133088964,
    0.7148465705529155,
    0.6308807679298587,
    -0.0279837694168599,
    -0.1870348117190931,
    0.0308413818355607,
    0.0328830116668852,
    -0.010597401785069,
]
REACH = 48
COEFS = 24
RIM = 16
NEED = 13
RANK = 21
BAND_ROWS = 56
VMEM = pltpu.VMEM
F32, BF16 = jnp.float32, jnp.bfloat16


def keys_weight(t):
    t = abs(t)
    if t <= 1.0:
        return 1.5 * t**3 - 2.5 * t**2 + 1.0
    return -0.5 * t**3 + 2.5 * t**2 - 4.0 * t + 2.0 if t < 2.0 else 0.0


def upsample_matrix(n):
    m = np.zeros((n, n // 4))
    for y in range(n):
        centre = (y + 0.5) / 4.0 - 0.5
        for k in range(int(np.floor(centre)) - 1, int(np.floor(centre)) + 3):
            m[y, k % (n // 4)] += keys_weight(centre - k)
    return m


def low_matrix(n, tree):
    taps, offset = (TAPS, 3) if tree == 0 else (TAPS[::-1], 4)
    m = np.zeros((n // 2, n))
    for k in range(n // 2):
        for j in range(8):
            m[k, (2 * k + j - offset) % n] += taps[j]
    return m


@functools.lru_cache(None)
def smooth_matrix(n, level):
    total = 0.0
    for tree in range(2):
        chain = np.eye(n)
        for step in range(level):
            chain = low_matrix(n >> step, tree) @ chain
        total = total + 0.5 * chain.T @ chain
    return total


def split_const(m):
    m = np.asarray(m, np.float32)
    hi = m.astype(BF16)
    lo = (m - hi.astype(np.float32)).astype(BF16)
    return hi, lo


@functools.lru_cache(None)
def constants(rows, cols):
    half = cols // 2
    n = 1024
    q = [smooth_matrix(n, level) for level in (1, 2, 3)]
    o = 256
    stack = lambda lo, hi: np.concatenate([m[o : o + 128, lo:hi] for m in q])
    send, recv = [], []
    for lo, hi in ((o - REACH, o), (o + 128, o + 128 + REACH)):
        _, s, vt = np.linalg.svd(stack(lo, hi), full_matrices=False)
        assert s[COEFS - 3] < 1e-14
        send.append(vt[:COEFS])
        recv.append(vt[:COEFS].T)
    below, above = send[0], send[1]
    own, edge = [], ([], [])
    for m in q:
        body = m[o : o + rows]
        own.append(body[:, o : o + rows])
        edge[0].append(body[:REACH, o - REACH : o] @ recv[0])
        edge[1].append(body[-REACH:, o + rows : o + rows + REACH] @ recv[1])
    c1, c2 = [], []
    for m in q:
        body = m[o : o + half]
        c1.append(body[:, o : o + half].T)
        left, right = body[:, o - REACH : o], body[:, o + half : o + half + REACH]
        nothing = np.zeros((half, COEFS))
        first = np.concatenate([left @ recv[0], nothing, right], 1).T
        second = np.concatenate([nothing, right @ recv[1], left], 1).T
        c2.append((first, second))
    qu = q[2] @ upsample_matrix(n)
    p = o // 4
    low = rows // 4
    cu = np.concatenate(
        [
            qu[o : o + cols, p : p + cols // 4],
            qu[o : o + cols, p - RIM : p],
            qu[o : o + cols, p + cols // 4 : p + cols // 4 + RIM],
        ],
        1,
    ).T
    ru = qu[o : o + rows]
    ru_own, ru_rims = ru[:, p : p + low], (ru[:, p - RIM : p], ru[:, p + low : p + low + RIM])
    ru_ends = (ru_rims[0][:BAND_ROWS], ru_rims[1][rows - BAND_ROWS :])
    assert not ru_rims[0][BAND_ROWS:].any() and not ru_rims[1][: rows - BAND_ROWS].any()

    def three(m):
        hi, lo = split_const(m)
        return np.concatenate([hi, hi, lo], 1)

    pair = lambda m: np.concatenate(split_const(m), 1)
    parts = dict(below=pair(below), above=pair(above))
    for side in range(2):
        parts[f"edge{side}"] = np.concatenate([three(m) for m in edge[side]])
    for side in range(2):
        parts[f"ru{side}"] = three(np.concatenate([ru_own, ru_rims[side]], 1))
    for side in range(2):
        assert not (ru_rims[0][:, : RIM - NEED] if side == 0 else ru_rims[1][:, NEED:]).any()
        used = ru_ends[side][:, RIM - NEED :] if side == 0 else ru_ends[side][:, :NEED]
        parts[f"end{side}"] = three(np.pad(used, ((0, 0), (0, RIM - NEED))))
        gap = np.zeros((BAND_ROWS - REACH, COEFS))
        for level in range(LEVELS):
            m = edge[side][level]
            parts[f"fix{level}{side}"] = three(np.concatenate([m, gap] if side == 0 else [gap, m]))
    for level in range(LEVELS):
        parts[f"own{level}"] = pair(own[level])
        parts[f"c1{level}hi"], parts[f"c1{level}lo"] = split_const(c1[level])
        for h in range(2):
            parts[f"c2{level}{h}hi"], parts[f"c2{level}{h}lo"] = split_const(c2[level][h])
    for h in range(2):
        parts[f"cu{h}hi"], parts[f"cu{h}lo"] = split_const(cu[:, h * half : (h + 1) * half])
    table, where, at = [], {}, 0
    for name, m in parts.items():
        high = -(-m.shape[0] // 16) * 16
        table.append(np.pad(np.asarray(m, np.float32), ((0, high - m.shape[0]), (0, half - m.shape[1]))))
        where[name] = (at, m.shape)
        at += high
    table = np.concatenate(table).astype(BF16)
    return table, table[: where["edge0"][0]], where


class Table:
    def __init__(self, ref, where):
        self.ref, self.where = ref, where

    def __getitem__(self, name):
        at, (high, wide) = self.where[name]
        return self.ref[at : at + high, 0:wide]

    def pair(self, name):
        x = self[name]
        wide = x.shape[1] // 2
        return x[:, :wide], x[:, wide:]

    def side(self, name, below):
        (first, (high, wide)), (second, _) = self.where[name + "0"], self.where[name + "1"]
        at = pl.multiple_of(jnp.where(below, second, first), 16)
        return self.ref[pl.ds(at, high), 0:wide]

    def two(self, name):
        return self[name + "hi"], self[name + "lo"]


def swap_pairs(count):
    return [(i, i ^ 1) for i in range(count)]


def odd_pairs(count):
    return [(i, (i - 1) % count if i % 2 == 0 else (i + 1) % count) for i in range(count)]


def column_steps(count):
    if count == 4:
        return [
            ([(i, i ^ k) for i in range(4)], k != 2, lambda c, k=k: c ^ k, lambda c, k=k: c ^ k)
            for k in (1, 3, 2)
        ]
    return [
        (
            [(i, (i + k) % count) for i in range(count)],
            k in (1, count - 1),
            lambda c, k=k: lax.rem(c + k, count),
            lambda c, k=k: lax.rem(c + count - k, count),
        )
        for k in [1, count - 1] + list(range(2, count - 1))
    ]


def split(x):
    hi = x.astype(BF16)
    return hi, (x - hi.astype(F32)).astype(BF16)


def dot(a, b, dims=((1,), (0,))):
    return lax.dot_general(a, b, (dims, ((), ())), preferred_element_type=F32)


def dot3(a, b, dims=((1,), (0,))):
    return dot(a[0], b[0], dims) + dot(a[1], b[0], dims) + dot(a[0], b[1], dims)


def rows3(a, b):
    high = a[0].shape[0]
    both = dot(jnp.concatenate(a, 0), b[0])
    return both[:high] + both[high:] + dot(a[0], b[1])


def three_high(x):
    if x.shape[0] % 16:
        hi = x.astype(BF16).astype(F32)
        return jnp.concatenate([hi, x - hi, hi], 0).astype(BF16)
    hi, lo = split(x)
    return jnp.concatenate([hi, lo, hi], 0)


def lanes(shape):
    return lax.broadcasted_iota(jnp.int32, shape, 1)


def pack_chunk(out, ms_ref, to, count):
    bands, low = ms_ref.shape[0], ms_ref.shape[1]
    main = bands * low
    block = lambda k: pl.ds(pl.multiple_of(lax.rem(k + count, count) * 128, 128), 128)
    packed = None
    for i in range(bands):
        out[i * low : (i + 1) * low, :] = ms_ref[i, :, block(to)]
        left, right = ms_ref[i, :, block(to - 1)], ms_ref[i, :, block(to + 1)]
        rim = jnp.where(lanes(left.shape) >= 64, left, right)
        for g in range(low // RIM):
            slot = i * (low // RIM) + g
            rolled = pltpu.roll(rim[g * RIM : (g + 1) * RIM], (2 * RIM * slot + RIM) % 128, 1)
            packed = rolled if slot == 0 else jnp.where(lanes(rolled.shape) >= 2 * RIM * slot, rolled, packed)
    out[main : main + RIM, :] = packed


def pack_kernel(count, where, ms_ref, first_ref, last_ref, table_ref, *out_refs):
    c = lax.axis_index("col")
    table = Table(table_ref, where)
    main = ms_ref.shape[0] * ms_ref.shape[1]
    below, above = table.pair("below"), table.pair("above")
    for step, out in zip(column_steps(count), out_refs):
        to = step[2](c)
        pack_chunk(out, ms_ref, to, count)
        if step[1]:
            to_right = to == lax.rem(c + 1, count)
            edge = jnp.where(to_right, pltpu.roll(last_ref[...], REACH, 1), first_ref[...])
            v = tuple(jnp.where(to_right, x.astype(F32), y.astype(F32)).astype(BF16) for x, y in zip(below, above))
            out[main + RIM : main + RIM + COEFS, :] = dot3(v, split(edge[:, :REACH]), ((1,), (1,)))


def stage_kernel(count, where, first, *refs):
    ms_hbm, pan_hbm, table_hbm, own_ref, top_ref, bot_ref, pan_ref, table_ref, ms_ref, sems = refs
    rest = table_ref.shape[0] - first
    moves = [
        (table_hbm.at[pl.ds(0, first)], table_ref.at[pl.ds(0, first)]),
        (pan_hbm, pan_ref),
        (ms_hbm, ms_ref),
        (table_hbm.at[pl.ds(first, rest)], table_ref.at[pl.ds(first, rest)]),
    ]
    copies = [pltpu.make_async_copy(x, y, sems.at[k]) for k, (x, y) in enumerate(moves)]
    for copy in copies:
        copy.start()
    for copy in copies[:3]:
        copy.wait()
    table = Table(table_ref, where)
    pack_chunk(own_ref, ms_ref, lax.axis_index("col"), count)
    rows = pan_ref.shape[0]
    for out, name, at in ((bot_ref, "below", rows - REACH), (top_ref, "above", 0)):
        full = dot3(table.pair(name), split(pan_ref[at : at + REACH, :]))
        for k in range(pan_ref.shape[1] // 128):
            out[k * COEFS : (k + 1) * COEFS, :] = full[:, k * 128 : (k + 1) * 128]
    copies[3].wait()


def rim_kernel(count, low, where, top_ref, bot_ref, table_ref, *refs):
    table = Table(table_ref, where)
    q = refs[:count]
    a_ref, b_ref, xh_ref = refs[count:]
    c, r = lax.axis_index("col"), lax.axis_index("row")
    steps = column_steps(count)
    bands = (q[0].shape[0] - RIM) // low
    main = bands * low
    even = lax.rem(r, 2) == 0
    first = q[1][main + RIM : main + RIM + COEFS, :]
    second = q[2][main + RIM : main + RIM + COEFS, :]
    first_is_right = steps[0][3](c) == lax.rem(c + 1, count)
    left = jnp.where(first_is_right, second, first)
    right = jnp.where(first_is_right, first, second)
    filler = jnp.zeros((128 - 2 * COEFS, 128), F32)
    xh = jnp.concatenate([left, right, filler], 0).T
    xh_ref[...] = xh
    height = top_ref.shape[0]
    per = low // RIM
    total = count * bands

    def fill(out, bottom, far):
        out[0:height, :] = (bot_ref if bottom else top_ref)[...]
        v = table.pair("below" if bottom else "above")
        corner = dot3(v, split(xh[xh.shape[0] - REACH :] if bottom else xh[:REACH]))
        if far:
            tight = jnp.where(lanes(corner.shape) < RANK, corner, pltpu.roll(corner, 128 - (COEFS - RANK), 1))
            packed = tight[0:8]
            for g in (1, 2):
                turned = pltpu.roll(tight[8 * g : 8 * g + 8], 2 * RANK * g, 1)
                packed = jnp.where(lanes(packed.shape) >= 2 * RANK * g, turned, packed)
            out[height : height + 8, :] = packed
        else:
            out[height : height + COEFS, :] = corner
        base = height + (8 if far else COEFS)
        rim_rows = NEED if far else RIM
        packed = None
        for n in range(total):
            ref, i = q[n // bands], n % bands
            row = (i + 1) * low - rim_rows if bottom else i * low
            out[base + n * rim_rows : base + (n + 1) * rim_rows, :] = ref[row : row + rim_rows, :]
            slot = per * (i + 1) - 1 if bottom else per * i
            rim = pltpu.roll(ref[main : main + RIM, :], (2 * RIM * (n % 4 - slot)) % 128, 1)
            packed = rim if n % 4 == 0 else jnp.where(lanes(rim.shape) >= 2 * RIM * (n % 4), rim, packed)
            if n % 4 == 3 or n == total - 1:
                spot = base + total * rim_rows + (n // 4) * rim_rows
                out[spot : spot + rim_rows, :] = packed[RIM - rim_rows :] if bottom else packed[:rim_rows]

    @pl.when(even)
    def _():
        fill(a_ref, 1, False)
        fill(b_ref, 0, True)

    @pl.when(jnp.logical_not(even))
    def _():
        fill(a_ref, 0, False)
        fill(b_ref, 1, True)


def own_rims(own_right, own_left, xh):
    inner = lanes(xh.shape) < 2 * COEFS
    return (
        jnp.where(inner, xh, pltpu.roll(own_right, 2 * COEFS, 1)),
        jnp.where(inner, xh, pltpu.roll(own_left, 2 * COEFS + REACH, 1)),
    )


def columns(x, cols, table, level):
    half = cols // 2
    high = x.shape[0]
    wide = 2 * COEFS + REACH
    main = rows3(split(jnp.concatenate([x[:, :half], x[:, half:cols]], 0)), table.two(f"c1{level}"))
    out = []
    for h in range(2):
        rim = split(x[:, cols + h * 128 : cols + h * 128 + wide])
        product = dot3 if high % 16 else rows3
        out.append(main[h * high : (h + 1) * high] + product(rim, table.two(f"c2{level}{h}")))
    return out


def low_columns(x_ref, y_ref, table):
    x = split(x_ref[:, 0 : 128 + 2 * RIM])
    half = y_ref.shape[1] // 2
    for h in range(2):
        y_ref[:, h * half : (h + 1) * half] = rows3(x, table.two(f"cu{h}"))


def fill_rows(xe, at, cols, piece, xh):
    blocks = cols // 128
    for k in range(blocks):
        xe[at, k * 128 : (k + 1) * 128] = piece(k)
    f, s = own_rims(piece(blocks // 2), piece(blocks // 2 - 1), xh)
    xe[at, cols : cols + 128] = f
    xe[at, cols + 128 : cols + 256] = s


def coef_piece(ref):
    return lambda k: ref[k * COEFS : (k + 1) * COEFS, :]


def band_rims(mext, ref, total, base, high, skip, rim_rows=RIM):
    filler = [jnp.zeros((RIM - rim_rows, 128), F32)] if rim_rows < RIM else []
    whole = lambda x: jnp.concatenate([x] + filler, 0) if filler else x
    for n in range(total):
        at = slice(n * high + skip, n * high + skip + RIM)
        mext[at, 0:128] = whole(ref[base + n * rim_rows : base + (n + 1) * rim_rows, :])
        spot = base + total * rim_rows + (n // 4) * rim_rows
        mext[at, 128:256] = pltpu.roll(whole(ref[spot : spot + rim_rows, :]), (-2 * RIM * (n % 4)) % 128, 1)


def local_kernel(count, low, where, gains_ref, *refs):
    q, refs = refs[:count], refs[count:]
    pan_ref, xh_ref, a_ref, table_ref, part_ref, gains_out, xe, tr, e3, mext, y_ref = refs
    table = Table(table_ref, where)
    c, r = lax.axis_index("col"), lax.axis_index("row")
    below = lax.rem(r, 2) == 0
    steps = column_steps(count)
    bands = (q[0].shape[0] - RIM) // low
    total = count * bands
    main = bands * low
    rows, cols = pan_ref.shape
    half = cols // 2
    per = low // RIM
    high = low + RIM
    for n in range(total):
        ref, i = q[n // bands], n % bands
        mext[n * high : n * high + low, 0:128] = ref[i * low : (i + 1) * low, :]
        for g in range(per):
            at = n * high + g * RIM
            mext[at : at + RIM, 128:256] = pltpu.roll(
                ref[main : main + RIM, :], (-2 * RIM * (i * per + g)) % 128, 1
            )
    band_rims(mext, a_ref, total, (cols // 128 + 1) * COEFS, high, low)
    low_columns(mext, y_ref, table)
    fill_rows(xe, slice(0, rows), cols, lambda k: pan_ref[:, k * 128 : (k + 1) * 128], xh_ref[...])
    fill_rows(xe, slice(rows, rows + COEFS), cols, coef_piece(a_ref), a_ref[cols // 128 * COEFS : (cols // 128 + 1) * COEFS, :])
    hi, lo = split(xe[0:rows, :])
    both = jnp.concatenate([hi, lo], 0)
    before = [None, None]
    added = dot(table.side("edge", below), three_high(xe[rows : rows + COEFS, :]))
    for level in range(LEVELS):
        ohi, olo = table.pair(f"own{level}")
        tr[level] = dot(jnp.concatenate([ohi, ohi], 1), both) + dot(olo, hi)
        at = pl.ds(pl.multiple_of(jnp.where(below, rows - REACH, 0), 16), REACH)
        tr[level, at, :] = tr[level, at, :] + added[level * REACH : (level + 1) * REACH]
        for h, e in enumerate(columns(tr[level], cols, table, level)):
            hs = slice(h * half, (h + 1) * half)
            e3[level, :, hs] = (pan_ref[:, hs] if level == 0 else before[h]) - e
            before[h] = e
    for j in range(count):
        src = c if j == 0 else steps[j - 1][3](c)
        for i in range(bands):
            n = j * bands + i
            band = src * bands + i
            g1, g2, g3 = gains_ref[band, 0], gains_ref[band, 1], gains_ref[band, 2]
            for k, g in enumerate((g1, g2, g3)):
                gains_out[3 * n + k : 3 * n + k + 1, :] = jnp.full((1, cols), g, F32)
            part_ref[n] = (
                dot(table.side("ru", below), three_high(y_ref[n * high : (n + 1) * high, :]))
                + g1 * e3[0]
                + g2 * e3[1]
                + g3 * e3[2]
            )


def main_kernel(count, bands, where, *refs):
    part_ref, gains_ref, b_ref, table_ref, out_ref, xe, de, mext, y_ref, obuf, sems = refs
    table = Table(table_ref, where)
    c, r = lax.axis_index("col"), lax.axis_index("row")
    steps = column_steps(count)
    below = lax.rem(r, 2) == 1
    total, rows, cols = part_ref.shape
    half = cols // 2
    blocks = cols // 128
    source = [c if j == 0 else steps[j - 1][3](c) for j in range(count)]
    band = [source[n // bands] * bands + n % bands for n in range(total)]
    done = pl.ds(pl.multiple_of(jnp.where(below, 0, BAND_ROWS), 8), rows - BAND_ROWS)
    late = pl.ds(pl.multiple_of(jnp.where(below, rows - BAND_ROWS, 0), 8), BAND_ROWS)
    copies = [
        pltpu.make_async_copy(part_ref.at[n, done], out_ref.at[band[n], done], sems.at[0, n])
        for n in range(total)
    ]
    for copy in copies:
        copy.start()
    height = blocks * COEFS
    band_rims(mext, b_ref, total, height + 8, RIM, 0, NEED)
    low_columns(mext, y_ref, table)
    packed = b_ref[height : height + 8, :]
    tight = jnp.concatenate([pltpu.roll(packed, (-2 * RANK * g) % 128, 1) for g in range(3)], 0)
    corner = jnp.where(lanes(tight.shape) < COEFS, tight, pltpu.roll(tight, COEFS - RANK, 1))
    fill_rows(xe, slice(0, COEFS), cols, coef_piece(b_ref), corner)
    before = [None, None]
    for level in range(LEVELS):
        for h, z in enumerate(columns(xe[...], cols, table, level)):
            fix = dot(table.side(f"fix{level}", below), three_high(z))
            de[level, :, h * half : (h + 1) * half] = -fix if level == 0 else before[h] - fix
            before[h] = fix
    for n in range(total):
        g = [gains_ref[3 * n + k : 3 * n + k + 1, :] for k in range(LEVELS)]
        obuf[n] = (
            part_ref[n, late, :]
            + dot(table.side("end", below), three_high(y_ref[n * RIM : (n + 1) * RIM, :]))
            + g[0] * de[0]
            + g[1] * de[1]
            + g[2] * de[2]
        )
        copy = pltpu.make_async_copy(obuf.at[n], out_ref.at[band[n], late], sems.at[1, n])
        copy.start()
        copies.append(copy)
    for copy in copies:
        copy.wait()


def on_device(multispectral, panchromatic, band_gains):
    count, row_count = lax.axis_size("col"), lax.axis_size("row")
    bands, low, _ = multispectral.shape
    rows, cols = panchromatic.shape
    total = count * bands
    table, small, where = constants(rows, cols)
    steps = column_steps(count)
    chunk = bands * low + RIM
    shape = lambda n, m=128: jax.ShapeDtypeStruct((n, m), F32)
    whole = pl.BlockSpec(memory_space=VMEM)
    heights = [chunk + (COEFS if step[1] else 0) for step in steps]
    last = cols // 128 - 1
    packed = pl.pallas_call(
        functools.partial(pack_kernel, count, where),
        out_shape=[pltpu.VMEM((h, 128), F32) for h in heights],
        grid=(1,),
        in_specs=[
            pl.BlockSpec(multispectral.shape, lambda i: (0, 0, 0)),
            pl.BlockSpec((rows, 128), lambda i: (0, 0)),
            pl.BlockSpec((rows, 128), lambda i: (0, last)),
            pl.BlockSpec(small.shape, lambda i: (0, 0)),
        ],
        out_specs=[whole for h in heights],
        name="pack",
    )(*(pltpu.with_memory_space_constraint(x, pltpu.HBM) for x in (multispectral, panchromatic, panchromatic, jnp.asarray(small))))
    params = lambda mib: pltpu.CompilerParams(vmem_limit_bytes=mib << 20)
    cost = lambda flops: pl.CostEstimate(flops=flops, bytes_accessed=10**6, transcendentals=0)
    table = jnp.asarray(table)
    height = cols // 128 * COEFS
    first = small.shape[0]
    in_hbm = lambda *xs: [pltpu.with_memory_space_constraint(x, pltpu.HBM) for x in xs]
    own, top, bot, pan, table = pl.pallas_call(
        functools.partial(stage_kernel, count, where, first),
        out_shape=[
            VMEM((chunk, 128), F32),
            VMEM((height, 128), F32),
            VMEM((height, 128), F32),
            VMEM((rows, cols), F32),
            VMEM(table.shape, BF16),
        ],
        in_specs=[pl.BlockSpec(memory_space=pltpu.HBM)] * 3,
        out_specs=[whole] * 5,
        scratch_shapes=[VMEM(multispectral.shape, F32), pltpu.SemaphoreType.DMA((4,))],
        compiler_params=params(8),
        cost_estimate=cost(10**9),
        name="stage",
    )(*in_hbm(multispectral, panchromatic, table))
    q = [own]
    for x, step in zip(packed, steps):
        q.append(lax.ppermute(x, "col", step[0]))
    sent = lambda corner, rim: height + corner + total * rim + -(-total // 4) * rim
    a, b, xh = pl.pallas_call(
        functools.partial(rim_kernel, count, low, where),
        out_shape=[shape(sent(COEFS, RIM)), shape(sent(8, NEED)), shape(rows)],
        in_specs=[whole] * (3 + count),
        out_specs=[whole] * 3,
        compiler_params=params(8),
        name="rim",
    )(top, bot, table, *q)
    a = lax.ppermute(a, "row", swap_pairs(row_count))
    b = lax.ppermute(b, "row", odd_pairs(row_count))
    smem = pl.BlockSpec(memory_space=pltpu.SMEM)
    part, scaled = pl.pallas_call(
        functools.partial(local_kernel, count, low, where),
        out_shape=[jax.ShapeDtypeStruct((total, rows, cols), F32), shape(LEVELS * total, cols)],
        in_specs=[smem] + [whole] * (count + 4),
        out_specs=[whole] * 2,
        scratch_shapes=[
            VMEM((rows + COEFS, cols + 256), F32),
            VMEM((LEVELS, rows, cols + 256), F32),
            VMEM((LEVELS, rows, cols), F32),
            VMEM((total * (low + RIM), 256), F32),
            VMEM((total * (low + RIM), cols), F32),
        ],
        compiler_params=params(16),
        cost_estimate=cost(4 * 10**9),
        name="local",
    )(band_gains, *q, pan, xh, a, table)
    return pl.pallas_call(
        functools.partial(main_kernel, count, bands, where),
        out_shape=jax.ShapeDtypeStruct((total, rows, cols), F32),
        in_specs=[whole] * 4,
        out_specs=pl.BlockSpec(memory_space=pltpu.HBM),
        scratch_shapes=[
            VMEM((COEFS, cols + 256), F32),
            VMEM((LEVELS, BAND_ROWS, cols), F32),
            VMEM((total * RIM, 256), F32),
            VMEM((total * RIM, cols), F32),
            VMEM((total, BAND_ROWS, cols), F32),
            pltpu.SemaphoreType.DMA((2, total)),
        ],
        compiler_params=params(16),
        name="combine",
    )(part, scaled, b, table)


def solution(mesh):
    in_specs = (P("col", "row", None), P("row", "col"), P())
    out_specs = P(None, "row", "col")
    return jax.shard_map(
        on_device, mesh=mesh, in_specs=in_specs, out_specs=out_specs, check_vma=False
    )
```

```python
import functools

import jax
import jax.numpy as jnp
import numpy as np
from jax import lax
from jax.experimental import pallas as pl
from jax.experimental.pallas import tpu as pltpu
from jax.sharding import PartitionSpec as P

LEVELS = 3
TAPS = [
    0.2303778133088964,
    0.7148465705529155,
    0.6308807679298587,
    -0.0279837694168599,
    -0.1870348117190931,
    0.0308413818355607,
    0.0328830116668852,
    -0.010597401785069,
]
REACH = 48
COEFS = 24
RIM = 16
NEED = 13
RANK = 21
BAND_ROWS = 56
VMEM = pltpu.VMEM
F32, BF16 = jnp.float32, jnp.bfloat16


def keys_weight(t):
    t = abs(t)
    if t <= 1.0:
        return 1.5 * t**3 - 2.5 * t**2 + 1.0
    return -0.5 * t**3 + 2.5 * t**2 - 4.0 * t + 2.0 if t < 2.0 else 0.0


def upsample_matrix(n):
    m = np.zeros((n, n // 4))
    for y in range(n):
        centre = (y + 0.5) / 4.0 - 0.5
        for k in range(int(np.floor(centre)) - 1, int(np.floor(centre)) + 3):
            m[y, k % (n // 4)] += keys_weight(centre - k)
    return m


def low_matrix(n, tree):
    taps, offset = (TAPS, 3) if tree == 0 else (TAPS[::-1], 4)
    m = np.zeros((n // 2, n))
    for k in range(n // 2):
        for j in range(8):
            m[k, (2 * k + j - offset) % n] += taps[j]
    return m


@functools.lru_cache(None)
def smooth_matrix(n, level):
    total = 0.0
    for tree in range(2):
        chain = np.eye(n)
        for step in range(level):
            chain = low_matrix(n >> step, tree) @ chain
        total = total + 0.5 * chain.T @ chain
    return total


def split_const(m):
    m = np.asarray(m, np.float32)
    hi = m.astype(BF16)
    lo = (m - hi.astype(np.float32)).astype(BF16)
    return hi, lo


@functools.lru_cache(None)
def constants(rows, cols):
    half = cols // 2
    n = 1024
    q = [smooth_matrix(n, level) for level in (1, 2, 3)]
    o = 256
    stack = lambda lo, hi: np.concatenate([m[o : o + 128, lo:hi] for m in q])
    send, recv = [], []
    for lo, hi in ((o - REACH, o), (o + 128, o + 128 + REACH)):
        _, s, vt = np.linalg.svd(stack(lo, hi), full_matrices=False)
        assert s[COEFS - 3] < 1e-14
        send.append(vt[:COEFS])
        recv.append(vt[:COEFS].T)
    below, above = send[0], send[1]
    own, edge = [], ([], [])
    for m in q:
        body = m[o : o + rows]
        own.append(body[:, o : o + rows])
        edge[0].append(body[:REACH, o - REACH : o] @ recv[0])
        edge[1].append(body[-REACH:, o + rows : o + rows + REACH] @ recv[1])
    c1, c2 = [], []
    for m in q:
        body = m[o : o + half]
        c1.append(body[:, o : o + half].T)
        left, right = body[:, o - REACH : o], body[:, o + half : o + half + REACH]
        nothing = np.zeros((half, COEFS))
        first = np.concatenate([left @ recv[0], nothing, right], 1).T
        second = np.concatenate([nothing, right @ recv[1], left], 1).T
        c2.append((first, second))
    qu = q[2] @ upsample_matrix(n)
    p = o // 4
    low = rows // 4
    cu = np.concatenate(
        [
            qu[o : o + cols, p : p + cols // 4],
            qu[o : o + cols, p - RIM : p],
            qu[o : o + cols, p + cols // 4 : p + cols // 4 + RIM],
        ],
        1,
    ).T
    ru = qu[o : o + rows]
    ru_own, ru_rims = ru[:, p : p + low], (ru[:, p - RIM : p], ru[:, p + low : p + low + RIM])
    ru_ends = (ru_rims[0][:BAND_ROWS], ru_rims[1][rows - BAND_ROWS :])
    assert not ru_rims[0][BAND_ROWS:].any() and not ru_rims[1][: rows - BAND_ROWS].any()

    def three(m):
        hi, lo = split_const(m)
        return np.concatenate([hi, hi, lo], 1)

    pair = lambda m: np.concatenate(split_const(m), 1)
    parts = dict(below=pair(below), above=pair(above))
    for side in range(2):
        parts[f"edge{side}"] = np.concatenate([three(m) for m in edge[side]])
    for side in range(2):
        parts[f"ru{side}"] = three(np.concatenate([ru_own, ru_rims[side]], 1))
    for side in range(2):
        assert not (ru_rims[0][:, : RIM - NEED] if side == 0 else ru_rims[1][:, NEED:]).any()
        used = ru_ends[side][:, RIM - NEED :] if side == 0 else ru_ends[side][:, :NEED]
        parts[f"end{side}"] = three(np.pad(used, ((0, 0), (0, RIM - NEED))))
        gap = np.zeros((BAND_ROWS - REACH, LEVELS * COEFS))
        m = np.concatenate(edge[side], 1)
        m = np.concatenate([m, gap] if side == 0 else [gap, m])
        for name, x in zip(("fixhi", "fixlo"), split_const(m)):
            parts[f"{name}{side}"] = np.concatenate([x] * 3, 1)
    for level in range(LEVELS):
        parts[f"own{level}"] = pair(own[level])
        parts[f"c1{level}hi"], parts[f"c1{level}lo"] = split_const(c1[level])
        for h in range(2):
            parts[f"c2{level}{h}hi"], parts[f"c2{level}{h}lo"] = split_const(c2[level][h])
    for h in range(2):
        parts[f"cu{h}hi"], parts[f"cu{h}lo"] = split_const(cu[:, h * half : (h + 1) * half])
    table, where, at = [], {}, 0
    for name, m in parts.items():
        high = -(-m.shape[0] // 16) * 16
        table.append(np.pad(np.asarray(m, np.float32), ((0, high - m.shape[0]), (0, half - m.shape[1]))))
        where[name] = (at, m.shape)
        at += high
    table = np.concatenate(table).astype(BF16)
    return table, table[: where["edge0"][0]], where


class Table:
    def __init__(self, ref, where):
        self.ref, self.where = ref, where

    def __getitem__(self, name):
        at, (high, wide) = self.where[name]
        return self.ref[at : at + high, 0:wide]

    def pair(self, name):
        x = self[name]
        wide = x.shape[1] // 2
        return x[:, :wide], x[:, wide:]

    def side(self, name, below):
        (first, (high, wide)), (second, _) = self.where[name + "0"], self.where[name + "1"]
        at = pl.multiple_of(jnp.where(below, second, first), 16)
        return self.ref[pl.ds(at, high), 0:wide]

    def two(self, name):
        return self[name + "hi"], self[name + "lo"]


def swap_pairs(count):
    return [(i, i ^ 1) for i in range(count)]


def odd_pairs(count):
    return [(i, (i - 1) % count if i % 2 == 0 else (i + 1) % count) for i in range(count)]


def column_steps(count):
    if count == 4:
        return [
            ([(i, i ^ k) for i in range(4)], k != 2, lambda c, k=k: c ^ k, lambda c, k=k: c ^ k)
            for k in (1, 3, 2)
        ]
    return [
        (
            [(i, (i + k) % count) for i in range(count)],
            k in (1, count - 1),
            lambda c, k=k: lax.rem(c + k, count),
            lambda c, k=k: lax.rem(c + count - k, count),
        )
        for k in [1, count - 1] + list(range(2, count - 1))
    ]


def split(x):
    hi = x.astype(BF16)
    return hi, (x - hi.astype(F32)).astype(BF16)


def dot(a, b, dims=((1,), (0,))):
    return lax.dot_general(a, b, (dims, ((), ())), preferred_element_type=F32)


def dot3(a, b, dims=((1,), (0,))):
    return dot(a[0], b[0], dims) + dot(a[1], b[0], dims) + dot(a[0], b[1], dims)


def rows3(a, b):
    high = a[0].shape[0]
    both = dot(jnp.concatenate(a, 0), b[0])
    return both[:high] + both[high:] + dot(a[0], b[1])


def three_high(x):
    if x.shape[0] % 16:
        hi = x.astype(BF16).astype(F32)
        return jnp.concatenate([hi, x - hi, hi], 0).astype(BF16)
    hi, lo = split(x)
    return jnp.concatenate([hi, lo, hi], 0)


def lanes(shape):
    return lax.broadcasted_iota(jnp.int32, shape, 1)


def pack_chunk(out, ms_ref, to, count):
    bands, low = ms_ref.shape[0], ms_ref.shape[1]
    main = bands * low
    block = lambda k: pl.ds(pl.multiple_of(lax.rem(k + count, count) * 128, 128), 128)
    packed = None
    for i in range(bands):
        out[i * low : (i + 1) * low, :] = ms_ref[i, :, block(to)]
        left, right = ms_ref[i, :, block(to - 1)], ms_ref[i, :, block(to + 1)]
        rim = jnp.where(lanes(left.shape) >= 64, left, right)
        for g in range(low // RIM):
            slot = i * (low // RIM) + g
            rolled = pltpu.roll(rim[g * RIM : (g + 1) * RIM], (2 * RIM * slot + RIM) % 128, 1)
            packed = rolled if slot == 0 else jnp.where(lanes(rolled.shape) >= 2 * RIM * slot, rolled, packed)
    out[main : main + RIM, :] = packed


def pack_kernel(count, where, ms_ref, first_ref, last_ref, table_ref, *out_refs):
    c = lax.axis_index("col")
    table = Table(table_ref, where)
    main = ms_ref.shape[0] * ms_ref.shape[1]
    below, above = table.pair("below"), table.pair("above")
    for step, out in zip(column_steps(count), out_refs):
        to = step[2](c)
        pack_chunk(out, ms_ref, to, count)
        if step[1]:
            to_right = to == lax.rem(c + 1, count)
            edge = jnp.where(to_right, pltpu.roll(last_ref[...], REACH, 1), first_ref[...])
            v = tuple(jnp.where(to_right, x.astype(F32), y.astype(F32)).astype(BF16) for x, y in zip(below, above))
            out[main + RIM : main + RIM + COEFS, :] = dot3(v, split(edge[:, :REACH]), ((1,), (1,)))


def stage_kernel(count, where, first, *refs):
    ms_hbm, pan_hbm, table_hbm, own_ref, top_ref, bot_ref, pan_ref, table_ref, ms_ref, sems = refs
    rest = table_ref.shape[0] - first
    moves = [
        (table_hbm.at[pl.ds(0, first)], table_ref.at[pl.ds(0, first)]),
        (pan_hbm, pan_ref),
        (ms_hbm, ms_ref),
        (table_hbm.at[pl.ds(first, rest)], table_ref.at[pl.ds(first, rest)]),
    ]
    copies = [pltpu.make_async_copy(x, y, sems.at[k]) for k, (x, y) in enumerate(moves)]
    for copy in copies:
        copy.start()
    for copy in copies[:3]:
        copy.wait()
    table = Table(table_ref, where)
    pack_chunk(own_ref, ms_ref, lax.axis_index("col"), count)
    rows = pan_ref.shape[0]
    for out, name, at in ((bot_ref, "below", rows - REACH), (top_ref, "above", 0)):
        full = dot3(table.pair(name), split(pan_ref[at : at + REACH, :]))
        for k in range(pan_ref.shape[1] // 128):
            out[k * COEFS : (k + 1) * COEFS, :] = full[:, k * 128 : (k + 1) * 128]
    copies[3].wait()


def rim_kernel(count, low, where, top_ref, bot_ref, table_ref, *refs):
    table = Table(table_ref, where)
    q = refs[:count]
    a_ref, b_ref, xh_ref = refs[count:]
    c, r = lax.axis_index("col"), lax.axis_index("row")
    steps = column_steps(count)
    bands = (q[0].shape[0] - RIM) // low
    main = bands * low
    even = lax.rem(r, 2) == 0
    first = q[1][main + RIM : main + RIM + COEFS, :]
    second = q[2][main + RIM : main + RIM + COEFS, :]
    first_is_right = steps[0][3](c) == lax.rem(c + 1, count)
    left = jnp.where(first_is_right, second, first)
    right = jnp.where(first_is_right, first, second)
    filler = jnp.zeros((128 - 2 * COEFS, 128), F32)
    xh = jnp.concatenate([left, right, filler], 0).T
    xh_ref[...] = xh
    height = top_ref.shape[0]
    per = low // RIM
    total = count * bands

    def fill(out, bottom, far):
        out[0:height, :] = (bot_ref if bottom else top_ref)[...]
        v = table.pair("below" if bottom else "above")
        corner = dot3(v, split(xh[xh.shape[0] - REACH :] if bottom else xh[:REACH]))
        if far:
            tight = jnp.where(lanes(corner.shape) < RANK, corner, pltpu.roll(corner, 128 - (COEFS - RANK), 1))
            packed = tight[0:8]
            for g in (1, 2):
                turned = pltpu.roll(tight[8 * g : 8 * g + 8], 2 * RANK * g, 1)
                packed = jnp.where(lanes(packed.shape) >= 2 * RANK * g, turned, packed)
            out[height : height + 8, :] = packed
        else:
            out[height : height + COEFS, :] = corner
        base = height + (8 if far else COEFS)
        rim_rows = NEED if far else RIM
        packed = None
        for n in range(total):
            ref, i = q[n // bands], n % bands
            row = (i + 1) * low - rim_rows if bottom else i * low
            out[base + n * rim_rows : base + (n + 1) * rim_rows, :] = ref[row : row + rim_rows, :]
            slot = per * (i + 1) - 1 if bottom else per * i
            rim = pltpu.roll(ref[main : main + RIM, :], (2 * RIM * (n % 4 - slot)) % 128, 1)
            packed = rim if n % 4 == 0 else jnp.where(lanes(rim.shape) >= 2 * RIM * (n % 4), rim, packed)
            if n % 4 == 3 or n == total - 1:
                spot = base + total * rim_rows + (n // 4) * rim_rows
                out[spot : spot + rim_rows, :] = packed[RIM - rim_rows :] if bottom else packed[:rim_rows]

    @pl.when(even)
    def _():
        fill(a_ref, 1, False)
        fill(b_ref, 0, True)

    @pl.when(jnp.logical_not(even))
    def _():
        fill(a_ref, 0, False)
        fill(b_ref, 1, True)


def own_rims(own_right, own_left, xh):
    inner = lanes(xh.shape) < 2 * COEFS
    return (
        jnp.where(inner, xh, pltpu.roll(own_right, 2 * COEFS, 1)),
        jnp.where(inner, xh, pltpu.roll(own_left, 2 * COEFS + REACH, 1)),
    )


def columns(x, cols, table, level):
    half = cols // 2
    high = x.shape[0]
    wide = 2 * COEFS + REACH
    main = rows3(split(jnp.concatenate([x[:, :half], x[:, half:cols]], 0)), table.two(f"c1{level}"))
    out = []
    for h in range(2):
        rim = split(x[:, cols + h * 128 : cols + h * 128 + wide])
        product = dot3 if high % 16 else rows3
        out.append(main[h * high : (h + 1) * high] + product(rim, table.two(f"c2{level}{h}")))
    return out


def low_columns(x_ref, y_ref, table):
    x = split(x_ref[:, 0 : 128 + 2 * RIM])
    half = y_ref.shape[1] // 2
    for h in range(2):
        y_ref[:, h * half : (h + 1) * half] = rows3(x, table.two(f"cu{h}"))


def fill_rows(xe, at, cols, piece, xh):
    blocks = cols // 128
    for k in range(blocks):
        xe[at, k * 128 : (k + 1) * 128] = piece(k)
    f, s = own_rims(piece(blocks // 2), piece(blocks // 2 - 1), xh)
    xe[at, cols : cols + 128] = f
    xe[at, cols + 128 : cols + 256] = s


def coef_piece(ref):
    return lambda k: ref[k * COEFS : (k + 1) * COEFS, :]


def band_rims(mext, ref, total, base, high, skip, rim_rows=RIM):
    filler = [jnp.zeros((RIM - rim_rows, 128), F32)] if rim_rows < RIM else []
    whole = lambda x: jnp.concatenate([x] + filler, 0) if filler else x
    for n in range(total):
        at = slice(n * high + skip, n * high + skip + RIM)
        mext[at, 0:128] = whole(ref[base + n * rim_rows : base + (n + 1) * rim_rows, :])
        spot = base + total * rim_rows + (n // 4) * rim_rows
        mext[at, 128:256] = pltpu.roll(whole(ref[spot : spot + rim_rows, :]), (-2 * RIM * (n % 4)) % 128, 1)


def local_kernel(count, low, where, gains_ref, *refs):
    q, refs = refs[:count], refs[count:]
    pan_ref, xh_ref, a_ref, table_ref, part_ref, fix_ref, xe, tr, e3, mext, y_ref = refs
    table = Table(table_ref, where)
    c, r = lax.axis_index("col"), lax.axis_index("row")
    below = lax.rem(r, 2) == 0
    steps = column_steps(count)
    bands = (q[0].shape[0] - RIM) // low
    total = count * bands
    main = bands * low
    rows, cols = pan_ref.shape
    half = cols // 2
    per = low // RIM
    high = low + RIM
    for n in range(total):
        ref, i = q[n // bands], n % bands
        mext[n * high : n * high + low, 0:128] = ref[i * low : (i + 1) * low, :]
        for g in range(per):
            at = n * high + g * RIM
            mext[at : at + RIM, 128:256] = pltpu.roll(
                ref[main : main + RIM, :], (-2 * RIM * (i * per + g)) % 128, 1
            )
    band_rims(mext, a_ref, total, (cols // 128 + 1) * COEFS, high, low)
    low_columns(mext, y_ref, table)
    fill_rows(xe, slice(0, rows), cols, lambda k: pan_ref[:, k * 128 : (k + 1) * 128], xh_ref[...])
    fill_rows(xe, slice(rows, rows + COEFS), cols, coef_piece(a_ref), a_ref[cols // 128 * COEFS : (cols // 128 + 1) * COEFS, :])
    hi, lo = split(xe[0:rows, :])
    both = jnp.concatenate([hi, lo], 0)
    before = [None, None]
    added = dot(table.side("edge", below), three_high(xe[rows : rows + COEFS, :]))
    for level in range(LEVELS):
        ohi, olo = table.pair(f"own{level}")
        tr[level] = dot(jnp.concatenate([ohi, ohi], 1), both) + dot(olo, hi)
        at = pl.ds(pl.multiple_of(jnp.where(below, rows - REACH, 0), 16), REACH)
        tr[level, at, :] = tr[level, at, :] + added[level * REACH : (level + 1) * REACH]
        for h, e in enumerate(columns(tr[level], cols, table, level)):
            hs = slice(h * half, (h + 1) * half)
            e3[level, :, hs] = (pan_ref[:, hs] if level == 0 else before[h]) - e
            before[h] = e
    far_below = jnp.logical_not(below)
    fix = table.side("fixhi", far_below).astype(F32) + table.side("fixlo", far_below).astype(F32)
    lane = lanes((1, fix.shape[1]))
    level_of = lax.rem(lane, LEVELS * COEFS) // COEFS
    first_two = lanes(fix.shape) < 2 * LEVELS * COEFS
    for j in range(count):
        src = c if j == 0 else steps[j - 1][3](c)
        for i in range(bands):
            n = j * bands + i
            band = src * bands + i
            g1, g2, g3 = gains_ref[band, 0], gains_ref[band, 1], gains_ref[band, 2]
            factor = jnp.where(level_of == 0, g2 - g1, jnp.where(level_of == 1, g3 - g2, -g3))
            scaled = factor * fix
            hi = scaled.astype(BF16).astype(F32)
            fix_ref[n * BAND_ROWS : (n + 1) * BAND_ROWS, :] = jnp.where(first_two, hi, scaled - hi)
            part_ref[n] = (
                dot(table.side("ru", below), three_high(y_ref[n * high : (n + 1) * high, :]))
                + g1 * e3[0]
                + g2 * e3[1]
                + g3 * e3[2]
            )


def main_kernel(count, bands, where, *refs):
    part_ref, fix_ref, b_ref, table_ref, out_ref, xe, mext, y_ref, obuf, sems = refs
    table = Table(table_ref, where)
    c, r = lax.axis_index("col"), lax.axis_index("row")
    steps = column_steps(count)
    below = lax.rem(r, 2) == 1
    total, rows, cols = part_ref.shape
    half = cols // 2
    blocks = cols // 128
    source = [c if j == 0 else steps[j - 1][3](c) for j in range(count)]
    band = [source[n // bands] * bands + n % bands for n in range(total)]
    done = pl.ds(pl.multiple_of(jnp.where(below, 0, BAND_ROWS), 8), rows - BAND_ROWS)
    late = pl.ds(pl.multiple_of(jnp.where(below, rows - BAND_ROWS, 0), 8), BAND_ROWS)
    copies = [
        pltpu.make_async_copy(part_ref.at[n, done], out_ref.at[band[n], done], sems.at[0, n])
        for n in range(total)
    ]

    @pl.loop(0, total)
    def _(k):
        at = sum(jnp.where(k == n, band[n], 0) for n in range(total))
        pltpu.make_async_copy(part_ref.at[k, done], out_ref.at[at, done], sems.at[0, k]).start()

    height = blocks * COEFS
    band_rims(mext, b_ref, total, height + 8, RIM, 0, NEED)
    low_columns(mext, y_ref, table)
    packed = b_ref[height : height + 8, :]
    tight = jnp.concatenate([pltpu.roll(packed, (-2 * RANK * g) % 128, 1) for g in range(3)], 0)
    corner = jnp.where(lanes(tight.shape) < COEFS, tight, pltpu.roll(tight, COEFS - RANK, 1))
    fill_rows(xe, slice(0, COEFS), cols, coef_piece(b_ref), corner)
    x = xe[...]
    levels = lambda name: tuple(
        jnp.concatenate([table.two(name(level))[k] for level in range(LEVELS)], 1) for k in range(2)
    )
    z = rows3(split(jnp.concatenate([x[:, :half], x[:, half:cols]], 0)), levels(lambda level: f"c1{level}"))
    wide = 2 * COEFS + REACH
    parts = []
    for h in range(2):
        rim = split(x[:, cols + h * 128 : cols + h * 128 + wide])
        parts.append(z[h * COEFS : (h + 1) * COEFS] + dot3(rim, levels(lambda level: f"c2{level}{h}")))
    stacked = [
        jnp.concatenate([p[:, level * half : (level + 1) * half] for p in parts], 1) for level in range(LEVELS)
    ]
    z = three_high(jnp.concatenate(stacked, 0))
    fix = dot(fix_ref[...].astype(BF16), z)
    for n in range(total):
        rim = three_high(y_ref[n * RIM : (n + 1) * RIM, :])
        add = dot(table.side("end", below), rim) + fix[n * BAND_ROWS : (n + 1) * BAND_ROWS]
        obuf[n] = part_ref[n, late, :] + add
        copy = pltpu.make_async_copy(obuf.at[n], out_ref.at[band[n], late], sems.at[1, n])
        copy.start()
        copies.append(copy)
    for copy in copies:
        copy.wait()


def on_device(multispectral, panchromatic, band_gains):
    count, row_count = lax.axis_size("col"), lax.axis_size("row")
    bands, low, _ = multispectral.shape
    rows, cols = panchromatic.shape
    total = count * bands
    table, small, where = constants(rows, cols)
    steps = column_steps(count)
    chunk = bands * low + RIM
    shape = lambda n, m=128: jax.ShapeDtypeStruct((n, m), F32)
    whole = pl.BlockSpec(memory_space=VMEM)
    heights = [chunk + (COEFS if step[1] else 0) for step in steps]
    last = cols // 128 - 1
    packed = pl.pallas_call(
        functools.partial(pack_kernel, count, where),
        out_shape=[pltpu.VMEM((h, 128), F32) for h in heights],
        grid=(1,),
        in_specs=[
            pl.BlockSpec(multispectral.shape, lambda i: (0, 0, 0)),
            pl.BlockSpec((rows, 128), lambda i: (0, 0)),
            pl.BlockSpec((rows, 128), lambda i: (0, last)),
            pl.BlockSpec(small.shape, lambda i: (0, 0)),
        ],
        out_specs=[whole for h in heights],
        name="pack",
    )(*(pltpu.with_memory_space_constraint(x, pltpu.HBM) for x in (multispectral, panchromatic, panchromatic, jnp.asarray(small))))
    params = lambda mib: pltpu.CompilerParams(vmem_limit_bytes=mib << 20)
    cost = lambda flops: pl.CostEstimate(flops=flops, bytes_accessed=10**6, transcendentals=0)
    table = jnp.asarray(table)
    height = cols // 128 * COEFS
    first = small.shape[0]
    in_hbm = lambda *xs: [pltpu.with_memory_space_constraint(x, pltpu.HBM) for x in xs]
    own, top, bot, pan, table = pl.pallas_call(
        functools.partial(stage_kernel, count, where, first),
        out_shape=[
            VMEM((chunk, 128), F32),
            VMEM((height, 128), F32),
            VMEM((height, 128), F32),
            VMEM((rows, cols), F32),
            VMEM(table.shape, BF16),
        ],
        in_specs=[pl.BlockSpec(memory_space=pltpu.HBM)] * 3,
        out_specs=[whole] * 5,
        scratch_shapes=[VMEM(multispectral.shape, F32), pltpu.SemaphoreType.DMA((4,))],
        compiler_params=params(8),
        cost_estimate=cost(10**9),
        name="stage",
    )(*in_hbm(multispectral, panchromatic, table))
    q = [own]
    for x, step in zip(packed, steps):
        q.append(lax.ppermute(x, "col", step[0]))
    sent = lambda corner, rim: height + corner + total * rim + -(-total // 4) * rim
    a, b, xh = pl.pallas_call(
        functools.partial(rim_kernel, count, low, where),
        out_shape=[shape(sent(COEFS, RIM)), shape(sent(8, NEED)), shape(rows)],
        in_specs=[whole] * (3 + count),
        out_specs=[whole] * 3,
        compiler_params=params(8),
        name="rim",
    )(top, bot, table, *q)
    a = lax.ppermute(a, "row", swap_pairs(row_count))
    b = lax.ppermute(b, "row", odd_pairs(row_count))
    smem = pl.BlockSpec(memory_space=pltpu.SMEM)
    part, scaled = pl.pallas_call(
        functools.partial(local_kernel, count, low, where),
        out_shape=[
            jax.ShapeDtypeStruct((total, rows, cols), F32),
            shape(total * BAND_ROWS, 3 * LEVELS * COEFS),
        ],
        in_specs=[smem] + [whole] * (count + 4),
        out_specs=[whole] * 2,
        scratch_shapes=[
            VMEM((rows + COEFS, cols + 256), F32),
            VMEM((LEVELS, rows, cols + 256), F32),
            VMEM((LEVELS, rows, cols), F32),
            VMEM((total * (low + RIM), 256), F32),
            VMEM((total * (low + RIM), cols), F32),
        ],
        compiler_params=params(16),
        cost_estimate=cost(4 * 10**9),
        name="local",
    )(band_gains, *q, pan, xh, a, table)
    return pl.pallas_call(
        functools.partial(main_kernel, count, bands, where),
        out_shape=jax.ShapeDtypeStruct((total, rows, cols), F32),
        in_specs=[whole] * 4,
        out_specs=pl.BlockSpec(memory_space=pltpu.HBM),
        scratch_shapes=[
            VMEM((COEFS, cols + 256), F32),
            VMEM((total * RIM, 256), F32),
            VMEM((total * RIM, cols), F32),
            VMEM((total, BAND_ROWS, cols), F32),
            pltpu.SemaphoreType.DMA((2, total)),
        ],
        compiler_params=params(16),
        name="combine",
    )(part, scaled, b, table)


def solution(mesh):
    in_specs = (P("col", "row", None), P("row", "col"), P())
    out_specs = P(None, "row", "col")
    return jax.shard_map(
        on_device, mesh=mesh, in_specs=in_specs, out_specs=out_specs, check_vma=False
    )
```

```python
import functools

import jax
import jax.numpy as jnp
import numpy as np
from jax import lax
from jax.experimental import pallas as pl
from jax.experimental.pallas import tpu as pltpu
from jax.sharding import PartitionSpec as P

LEVELS = 3
TAPS = [
    0.2303778133088964,
    0.7148465705529155,
    0.6308807679298587,
    -0.0279837694168599,
    -0.1870348117190931,
    0.0308413818355607,
    0.0328830116668852,
    -0.010597401785069,
]
REACH = 48
COEFS = 24
RIM = 16
NEED = 13
RANK = 21
BAND_ROWS = 56
VMEM = pltpu.VMEM
F32, BF16 = jnp.float32, jnp.bfloat16


def keys_weight(t):
    t = abs(t)
    if t <= 1.0:
        return 1.5 * t**3 - 2.5 * t**2 + 1.0
    return -0.5 * t**3 + 2.5 * t**2 - 4.0 * t + 2.0 if t < 2.0 else 0.0


def upsample_matrix(n):
    m = np.zeros((n, n // 4))
    for y in range(n):
        centre = (y + 0.5) / 4.0 - 0.5
        for k in range(int(np.floor(centre)) - 1, int(np.floor(centre)) + 3):
            m[y, k % (n // 4)] += keys_weight(centre - k)
    return m


def low_matrix(n, tree):
    taps, offset = (TAPS, 3) if tree == 0 else (TAPS[::-1], 4)
    m = np.zeros((n // 2, n))
    for k in range(n // 2):
        for j in range(8):
            m[k, (2 * k + j - offset) % n] += taps[j]
    return m


@functools.lru_cache(None)
def smooth_matrix(n, level):
    total = 0.0
    for tree in range(2):
        chain = np.eye(n)
        for step in range(level):
            chain = low_matrix(n >> step, tree) @ chain
        total = total + 0.5 * chain.T @ chain
    return total


def split_const(m):
    m = np.asarray(m, np.float32)
    hi = m.astype(BF16)
    lo = (m - hi.astype(np.float32)).astype(BF16)
    return hi, lo


@functools.lru_cache(None)
def constants(rows, cols):
    half = cols // 2
    n = 1024
    q = [smooth_matrix(n, level) for level in (1, 2, 3)]
    o = 256
    stack = lambda lo, hi: np.concatenate([m[o : o + 128, lo:hi] for m in q])
    send, recv = [], []
    for lo, hi in ((o - REACH, o), (o + 128, o + 128 + REACH)):
        _, s, vt = np.linalg.svd(stack(lo, hi), full_matrices=False)
        assert s[COEFS - 3] < 1e-14
        send.append(vt[:COEFS])
        recv.append(vt[:COEFS].T)
    below, above = send[0], send[1]
    own, edge = [], ([], [])
    for m in q:
        body = m[o : o + rows]
        own.append(body[:, o : o + rows])
        edge[0].append(body[:REACH, o - REACH : o] @ recv[0])
        edge[1].append(body[-REACH:, o + rows : o + rows + REACH] @ recv[1])
    c1, c2 = [], []
    for m in q:
        body = m[o : o + half]
        c1.append(body[:, o : o + half].T)
        left, right = body[:, o - REACH : o], body[:, o + half : o + half + REACH]
        nothing = np.zeros((half, COEFS))
        first = np.concatenate([left @ recv[0], nothing, right], 1).T
        second = np.concatenate([nothing, right @ recv[1], left], 1).T
        c2.append((first, second))
    qu = q[2] @ upsample_matrix(n)
    p = o // 4
    low = rows // 4
    cu = np.concatenate(
        [
            qu[o : o + cols, p : p + cols // 4],
            qu[o : o + cols, p - RIM : p],
            qu[o : o + cols, p + cols // 4 : p + cols // 4 + RIM],
        ],
        1,
    ).T
    ru = qu[o : o + rows]
    ru_own, ru_rims = ru[:, p : p + low], (ru[:, p - RIM : p], ru[:, p + low : p + low + RIM])
    ru_ends = (ru_rims[0][:BAND_ROWS], ru_rims[1][rows - BAND_ROWS :])
    assert not ru_rims[0][BAND_ROWS:].any() and not ru_rims[1][: rows - BAND_ROWS].any()

    def three(m):
        hi, lo = split_const(m)
        return np.concatenate([hi, hi, lo], 1)

    pair = lambda m: np.concatenate(split_const(m), 1)
    parts = dict(below=pair(below), above=pair(above))
    for level in range(LEVELS):
        parts[f"own{level}"] = pair(own[level])
    for level in range(LEVELS):
        parts[f"c1{level}hi"], parts[f"c1{level}lo"] = split_const(c1[level])
    nothing = np.zeros((REACH, COEFS))
    for level in range(LEVELS):
        parts[f"edge{level}"] = three(np.block([[edge[0][level], nothing], [nothing, edge[1][level]]]))
    for side in range(2):
        parts[f"ru{side}"] = three(np.concatenate([ru_own, ru_rims[side]], 1))
    for side in range(2):
        assert not (ru_rims[0][:, : RIM - NEED] if side == 0 else ru_rims[1][:, NEED:]).any()
        used = ru_ends[side][:, RIM - NEED :] if side == 0 else ru_ends[side][:, :NEED]
        parts[f"end{side}"] = three(np.pad(used, ((0, 0), (0, RIM - NEED))))
        gap = np.zeros((BAND_ROWS - REACH, LEVELS * COEFS))
        m = np.concatenate(edge[side], 1)
        m = np.concatenate([m, gap] if side == 0 else [gap, m])
        for name, x in zip(("fixhi", "fixlo"), split_const(m)):
            parts[f"{name}{side}"] = np.concatenate([x] * 3, 1)
    for level in range(LEVELS):
        for h in range(2):
            parts[f"c2{level}{h}hi"], parts[f"c2{level}{h}lo"] = split_const(c2[level][h])
    for h in range(2):
        parts[f"cu{h}hi"], parts[f"cu{h}lo"] = split_const(cu[:, h * half : (h + 1) * half])
    table, where, at = [], {}, 0
    for name, m in parts.items():
        high = -(-m.shape[0] // 16) * 16
        table.append(np.pad(np.asarray(m, np.float32), ((0, high - m.shape[0]), (0, half - m.shape[1]))))
        where[name] = (at, m.shape)
        at += high
    table = np.concatenate(table).astype(BF16)
    return table, (where["own0"][0], where["edge0"][0]), where


class Table:
    def __init__(self, ref, where):
        self.ref, self.where = ref, where

    def __getitem__(self, name):
        at, (high, wide) = self.where[name]
        return self.ref[at : at + high, 0:wide]

    def pair(self, name):
        x = self[name]
        wide = x.shape[1] // 2
        return x[:, :wide], x[:, wide:]

    def side(self, name, below):
        (first, (high, wide)), (second, _) = self.where[name + "0"], self.where[name + "1"]
        at = pl.multiple_of(jnp.where(below, second, first), 16)
        return self.ref[pl.ds(at, high), 0:wide]

    def two(self, name):
        return self[name + "hi"], self[name + "lo"]


def swap_pairs(count):
    return [(i, i ^ 1) for i in range(count)]


def odd_pairs(count):
    return [(i, (i - 1) % count if i % 2 == 0 else (i + 1) % count) for i in range(count)]


def column_steps(count):
    if count == 4:
        return [
            ([(i, i ^ k) for i in range(4)], k != 2, lambda c, k=k: c ^ k, lambda c, k=k: c ^ k)
            for k in (1, 3, 2)
        ]
    return [
        (
            [(i, (i + k) % count) for i in range(count)],
            k in (1, count - 1),
            lambda c, k=k: lax.rem(c + k, count),
            lambda c, k=k: lax.rem(c + count - k, count),
        )
        for k in [1, count - 1] + list(range(2, count - 1))
    ]


def split(x):
    hi = x.astype(BF16)
    return hi, (x - hi.astype(F32)).astype(BF16)


def dot(a, b, dims=((1,), (0,))):
    return lax.dot_general(a, b, (dims, ((), ())), preferred_element_type=F32)


def dot3(a, b, dims=((1,), (0,))):
    return dot(a[0], b[0], dims) + dot(a[1], b[0], dims) + dot(a[0], b[1], dims)


def rows3(a, b):
    high = a[0].shape[0]
    both = dot(jnp.concatenate(a, 0), b[0])
    return both[:high] + both[high:] + dot(a[0], b[1])


def three_high(x):
    if x.shape[0] % 16:
        hi = x.astype(BF16).astype(F32)
        return jnp.concatenate([hi, x - hi, hi], 0).astype(BF16)
    hi, lo = split(x)
    return jnp.concatenate([hi, lo, hi], 0)


def lanes(shape):
    return lax.broadcasted_iota(jnp.int32, shape, 1)


def pack_chunk(out, ms_ref, to, count):
    bands, low = ms_ref.shape[0], ms_ref.shape[1]
    main = bands * low
    block = lambda k: pl.ds(pl.multiple_of(lax.rem(k + count, count) * 128, 128), 128)
    packed = None
    for i in range(bands):
        out[i * low : (i + 1) * low, :] = ms_ref[i, :, block(to)]
        left, right = ms_ref[i, :, block(to - 1)], ms_ref[i, :, block(to + 1)]
        rim = jnp.where(lanes(left.shape) >= 64, left, right)
        for g in range(low // RIM):
            slot = i * (low // RIM) + g
            rolled = pltpu.roll(rim[g * RIM : (g + 1) * RIM], (2 * RIM * slot + RIM) % 128, 1)
            packed = rolled if slot == 0 else jnp.where(lanes(rolled.shape) >= 2 * RIM * slot, rolled, packed)
    out[main : main + RIM, :] = packed


def pack_kernel(count, where, ms_ref, pan_ref, table_ref, *out_refs):
    c, r = lax.axis_index("col"), lax.axis_index("row")
    table = Table(table_ref, where)
    main = ms_ref.shape[0] * ms_ref.shape[1]
    rows, cols = pan_ref.shape
    below, above = table.pair("below"), table.pair("above")
    choose = lambda first: tuple(
        jnp.where(first, x.astype(F32), y.astype(F32)).astype(BF16) for x, y in zip(below, above)
    )
    for step, out in zip(column_steps(count), out_refs):
        to = step[2](c)
        pack_chunk(out, ms_ref, to, count)
        if step[1]:
            to_right = to == lax.rem(c + 1, count)
            edge = jnp.where(to_right, pltpu.roll(pan_ref[:, cols - 128 :], REACH, 1), pan_ref[:, :128])
            out[main + RIM : main + RIM + COEFS, :] = dot3(choose(to_right), split(edge[:, :REACH]), ((1,), (1,)))
    bottom = lax.rem(r, 2) == 1
    at = pl.multiple_of(jnp.where(bottom, rows - REACH, 0), 16)
    full = dot3(choose(bottom), split(pan_ref[pl.ds(at, REACH), :]))
    for k in range(cols // 128):
        out_refs[-1][k * COEFS : (k + 1) * COEFS, :] = full[:, k * 128 : (k + 1) * 128]


def stage_kernel(count, where, cuts, *refs):
    ms_hbm, pan_hbm, table_hbm = refs[:3]
    own_ref, top_ref, bot_ref, pan_ref, table_ref, e1, ms_ref, sems = refs[3:]
    ends = (0,) + cuts + (table_ref.shape[0],)
    parts = [pl.ds(x, y - x) for x, y in zip(ends, ends[1:])]
    moves = [(pan_hbm, pan_ref)] + [(table_hbm.at[x], table_ref.at[x]) for x in parts[:2]]
    moves += [(ms_hbm, ms_ref), (table_hbm.at[parts[2]], table_ref.at[parts[2]])]
    copies = [pltpu.make_async_copy(x, y, sems.at[k]) for k, (x, y) in enumerate(moves)]
    for copy in copies:
        copy.start()
    copies[0].wait()
    copies[1].wait()
    table = Table(table_ref, where)
    rows, cols = pan_ref.shape
    half = cols // 2
    for out, name, at in ((bot_ref, "below", rows - REACH), (top_ref, "above", 0)):
        full = dot3(table.pair(name), split(pan_ref[at : at + REACH, :]))
        for k in range(cols // 128):
            out[k * COEFS : (k + 1) * COEFS, :] = full[:, k * 128 : (k + 1) * 128]
    copies[2].wait()
    hi, lo = split(pan_ref[...])
    both = jnp.concatenate([hi, lo], 0)
    for level in range(LEVELS):
        t = dot(jnp.concatenate([table.pair(f"own{level}")[0]] * 2, 1), both) + dot(table.pair(f"own{level}")[1], hi)
        main = rows3(split(jnp.concatenate([t[:, :half], t[:, half:]], 0)), table.two(f"c1{level}"))
        e1[level, :, 0:half] = main[:rows]
        e1[level, :, half:] = main[rows:]
    copies[3].wait()
    pack_chunk(own_ref, ms_ref, lax.axis_index("col"), count)
    copies[4].wait()


def rim_kernel(count, low, where, top_ref, bot_ref, table_ref, *refs):
    table = Table(table_ref, where)
    q = refs[:count]
    a_ref, b_ref, xh_ref = refs[count:]
    c, r = lax.axis_index("col"), lax.axis_index("row")
    steps = column_steps(count)
    bands = (q[0].shape[0] - RIM) // low
    main = bands * low
    even = lax.rem(r, 2) == 0
    first = q[1][main + RIM : main + RIM + COEFS, :]
    second = q[2][main + RIM : main + RIM + COEFS, :]
    first_is_right = steps[0][3](c) == lax.rem(c + 1, count)
    left = jnp.where(first_is_right, second, first)
    right = jnp.where(first_is_right, first, second)
    filler = jnp.zeros((128 - 2 * COEFS, 128), F32)
    xh = jnp.concatenate([left, right, filler], 0).T
    xh_ref[...] = xh
    per = low // RIM
    total = count * bands

    def fill(out, bottom, far):
        height = 0 if far else top_ref.shape[0]
        if not far:
            out[0:height, :] = (bot_ref if bottom else top_ref)[...]
        v = table.pair("below" if bottom else "above")
        corner = dot3(v, split(xh[xh.shape[0] - REACH :] if bottom else xh[:REACH]))
        if far:
            tight = jnp.where(lanes(corner.shape) < RANK, corner, pltpu.roll(corner, 128 - (COEFS - RANK), 1))
            packed = tight[0:8]
            for g in (1, 2):
                turned = pltpu.roll(tight[8 * g : 8 * g + 8], 2 * RANK * g, 1)
                packed = jnp.where(lanes(packed.shape) >= 2 * RANK * g, turned, packed)
            out[height : height + 8, :] = packed
        else:
            out[height : height + COEFS, :] = corner
        base = height + (8 if far else COEFS)
        rim_rows = NEED if far else RIM
        packed = None
        for n in range(total):
            ref, i = q[n // bands], n % bands
            row = (i + 1) * low - rim_rows if bottom else i * low
            out[base + n * rim_rows : base + (n + 1) * rim_rows, :] = ref[row : row + rim_rows, :]
            slot = per * (i + 1) - 1 if bottom else per * i
            rim = pltpu.roll(ref[main : main + RIM, :], (2 * RIM * (n % 4 - slot)) % 128, 1)
            packed = rim if n % 4 == 0 else jnp.where(lanes(rim.shape) >= 2 * RIM * (n % 4), rim, packed)
            if n % 4 == 3 or n == total - 1:
                spot = base + total * rim_rows + (n // 4) * rim_rows
                out[spot : spot + rim_rows, :] = packed[RIM - rim_rows :] if bottom else packed[:rim_rows]

    @pl.when(even)
    def _():
        fill(a_ref, 1, False)
        fill(b_ref, 0, True)

    @pl.when(jnp.logical_not(even))
    def _():
        fill(a_ref, 0, False)
        fill(b_ref, 1, True)


def own_rims(own_right, own_left, xh):
    inner = lanes(xh.shape) < 2 * COEFS
    return (
        jnp.where(inner, xh, pltpu.roll(own_right, 2 * COEFS, 1)),
        jnp.where(inner, xh, pltpu.roll(own_left, 2 * COEFS + REACH, 1)),
    )


def columns(x, cols, table, level):
    half = cols // 2
    high = x.shape[0]
    wide = 2 * COEFS + REACH
    main = rows3(split(jnp.concatenate([x[:, :half], x[:, half:cols]], 0)), table.two(f"c1{level}"))
    out = []
    for h in range(2):
        rim = split(x[:, cols + h * 128 : cols + h * 128 + wide])
        product = dot3 if high % 16 else rows3
        out.append(main[h * high : (h + 1) * high] + product(rim, table.two(f"c2{level}{h}")))
    return out


def low_columns(x_ref, y_ref, table):
    x = split(x_ref[:, 0 : 128 + 2 * RIM])
    half = y_ref.shape[1] // 2
    for h in range(2):
        y_ref[:, h * half : (h + 1) * half] = rows3(x, table.two(f"cu{h}"))


def fill_rows(xe, at, cols, piece, xh):
    blocks = cols // 128
    for k in range(blocks):
        xe[at, k * 128 : (k + 1) * 128] = piece(k)
    f, s = own_rims(piece(blocks // 2), piece(blocks // 2 - 1), xh)
    xe[at, cols : cols + 128] = f
    xe[at, cols + 128 : cols + 256] = s


def coef_piece(ref):
    return lambda k: ref[k * COEFS : (k + 1) * COEFS, :]


def band_rims(mext, ref, total, base, high, skip, rim_rows=RIM):
    filler = [jnp.zeros((RIM - rim_rows, 128), F32)] if rim_rows < RIM else []
    whole = lambda x: jnp.concatenate([x] + filler, 0) if filler else x
    for n in range(total):
        at = slice(n * high + skip, n * high + skip + RIM)
        mext[at, 0:128] = whole(ref[base + n * rim_rows : base + (n + 1) * rim_rows, :])
        spot = base + total * rim_rows + (n // 4) * rim_rows
        mext[at, 128:256] = pltpu.roll(whole(ref[spot : spot + rim_rows, :]), (-2 * RIM * (n % 4)) % 128, 1)


def local_kernel(count, low, where, gains_ref, *refs):
    q, refs = refs[:count], refs[count:]
    pan_ref, xh_ref, a_ref, far_ref, e1, table_ref = refs[:6]
    part_ref, fix_ref, xr, xe, e3, mext, y_ref = refs[6:]
    table = Table(table_ref, where)
    c, r = lax.axis_index("col"), lax.axis_index("row")
    below = lax.rem(r, 2) == 0
    steps = column_steps(count)
    bands = (q[0].shape[0] - RIM) // low
    total = count * bands
    main = bands * low
    rows, cols = pan_ref.shape
    half = cols // 2
    per = low // RIM
    high = low + RIM
    for n in range(total):
        ref, i = q[n // bands], n % bands
        mext[n * high : n * high + low, 0:128] = ref[i * low : (i + 1) * low, :]
        for g in range(per):
            at = n * high + g * RIM
            mext[at : at + RIM, 128:256] = pltpu.roll(
                ref[main : main + RIM, :], (-2 * RIM * (i * per + g)) % 128, 1
            )
    band_rims(mext, a_ref, total, (cols // 128 + 1) * COEFS, high, low)
    low_columns(mext, y_ref, table)
    xr[:, 0:128], xr[:, 128:256] = own_rims(
        pan_ref[:, half : half + 128], pan_ref[:, half - 128 : half], xh_ref[...]
    )
    blocks = cols // 128
    at = lambda under: pl.ds(pl.multiple_of(jnp.where(under, COEFS, 0), 8), COEFS)
    fill_rows(xe, at(below), cols, coef_piece(a_ref), a_ref[blocks * COEFS : (blocks + 1) * COEFS, :])
    fill_rows(xe, at(jnp.logical_not(below)), cols, coef_piece(far_ref), jnp.zeros((COEFS, 128), F32))
    hi, lo = split(xr[...])
    both = jnp.concatenate([hi, lo], 0)
    wide = 2 * COEFS + REACH
    x = xe[...]
    before = [pan_ref[:, h * half : (h + 1) * half] for h in range(2)]
    for level in range(LEVELS):
        ohi, olo = table.pair(f"own{level}")
        t = dot(jnp.concatenate([ohi, ohi], 1), both) + dot(olo, hi)
        for h, z in enumerate(columns(x, cols, table, level)):
            hs = slice(h * half, (h + 1) * half)
            de = dot(table[f"edge{level}"], three_high(z))
            e = e1[level, :, hs] + rows3(split(t[:, h * 128 : h * 128 + wide]), table.two(f"c2{level}{h}"))
            e = jnp.concatenate([e[:REACH] + de[:REACH], e[REACH : rows - REACH], e[rows - REACH :] + de[REACH:]], 0)
            e3[level, :, hs] = before[h] - e
            before[h] = e
    far_below = jnp.logical_not(below)
    fix = table.side("fixhi", far_below).astype(F32) + table.side("fixlo", far_below).astype(F32)
    lane = lanes((1, fix.shape[1]))
    level_of = lax.rem(lane, LEVELS * COEFS) // COEFS
    first_two = lanes(fix.shape) < 2 * LEVELS * COEFS
    for j in range(count):
        src = c if j == 0 else steps[j - 1][3](c)
        for i in range(bands):
            n = j * bands + i
            band = src * bands + i
            g1, g2, g3 = gains_ref[0, band], gains_ref[1, band], gains_ref[2, band]
            factor = jnp.where(level_of == 0, g2 - g1, jnp.where(level_of == 1, g3 - g2, -g3))
            scaled = factor * fix
            hi = scaled.astype(BF16).astype(F32)
            fix_ref[n * BAND_ROWS : (n + 1) * BAND_ROWS, :] = jnp.where(first_two, hi, scaled - hi)
            part_ref[n] = (
                dot(table.side("ru", below), three_high(y_ref[n * high : (n + 1) * high, :]))
                + g1 * e3[0]
                + g2 * e3[1]
                + g3 * e3[2]
            )


def main_kernel(count, bands, where, *refs):
    part_ref, fix_ref, b_ref, table_ref, out_ref, mext, y_ref, obuf, sems = refs
    table = Table(table_ref, where)
    c, r = lax.axis_index("col"), lax.axis_index("row")
    steps = column_steps(count)
    below = lax.rem(r, 2) == 1
    total, rows, cols = part_ref.shape
    half = cols // 2
    source = [c if j == 0 else steps[j - 1][3](c) for j in range(count)]
    band = [source[n // bands] * bands + n % bands for n in range(total)]
    done = pl.ds(pl.multiple_of(jnp.where(below, 0, BAND_ROWS), 8), rows - BAND_ROWS)
    late = pl.ds(pl.multiple_of(jnp.where(below, rows - BAND_ROWS, 0), 8), BAND_ROWS)
    copies = [
        pltpu.make_async_copy(part_ref.at[n, done], out_ref.at[band[n], done], sems.at[0, n])
        for n in range(total)
    ]

    @pl.loop(0, total)
    def _(k):
        at = sum(jnp.where(k == n, band[n], 0) for n in range(total))
        pltpu.make_async_copy(part_ref.at[k, done], out_ref.at[at, done], sems.at[0, k]).start()

    band_rims(mext, b_ref, total, 8, RIM, 0, NEED)
    low_columns(mext, y_ref, table)
    packed = b_ref[0:8, :]
    tight = jnp.concatenate([pltpu.roll(packed, (-2 * RANK * g) % 128, 1) for g in range(3)], 0)
    corner = jnp.where(lanes(tight.shape) < COEFS, tight, pltpu.roll(tight, COEFS - RANK, 1))
    corner = split(corner[:, : 2 * COEFS])
    ends = []
    for h in range(2):
        lane = slice(0, 128) if h == 0 else slice(half - 128, half)
        rim = tuple(
            jnp.concatenate([table.two(f"c2{level}{h}")[k][: 2 * COEFS, lane] for level in range(LEVELS)], 1)
            for k in range(2)
        )
        ends.append(dot3(corner, rim))
    stacked = [jnp.concatenate([z[:, level * 128 : (level + 1) * 128] for z in ends], 1) for level in range(LEVELS)]
    fix = dot(fix_ref[...].astype(BF16), three_high(jnp.concatenate(stacked, 0)))
    for n in range(total):
        rim = three_high(y_ref[n * RIM : (n + 1) * RIM, :])
        base = part_ref[n, late, :] + dot(table.side("end", below), rim)
        add = fix[n * BAND_ROWS : (n + 1) * BAND_ROWS]
        obuf[n, :, 0:128] = base[:, 0:128] + add[:, 0:128]
        obuf[n, :, 128 : cols - 128] = base[:, 128 : cols - 128]
        obuf[n, :, cols - 128 :] = base[:, cols - 128 :] + add[:, 128:]
        copy = pltpu.make_async_copy(obuf.at[n], out_ref.at[band[n], late], sems.at[1, n])
        copy.start()
        copies.append(copy)
    for copy in copies:
        copy.wait()


def on_device(multispectral, panchromatic, band_gains):
    count, row_count = lax.axis_size("col"), lax.axis_size("row")
    bands, low, _ = multispectral.shape
    rows, cols = panchromatic.shape
    total = count * bands
    table, cuts, where = constants(rows, cols)
    small = table[: cuts[0]]
    steps = column_steps(count)
    chunk = bands * low + RIM
    shape = lambda n, m=128: jax.ShapeDtypeStruct((n, m), F32)
    whole = pl.BlockSpec(memory_space=VMEM)
    heights = [chunk + (COEFS if step[1] else 0) for step in steps]
    height = cols // 128 * COEFS
    in_hbm = lambda *xs: [pltpu.with_memory_space_constraint(x, pltpu.HBM) for x in xs]
    *packed, far = pl.pallas_call(
        functools.partial(pack_kernel, count, where),
        out_shape=[VMEM((h, 128), F32) for h in heights + [height]],
        grid=(1,),
        in_specs=[
            pl.BlockSpec(multispectral.shape, lambda i: (0, 0, 0)),
            pl.BlockSpec(panchromatic.shape, lambda i: (0, 0)),
            pl.BlockSpec(small.shape, lambda i: (0, 0)),
        ],
        out_specs=[whole] * (len(heights) + 1),
        compiler_params=pltpu.CompilerParams(vmem_limit_bytes=8 << 20),
        name="pack",
    )(*in_hbm(multispectral, panchromatic, jnp.asarray(small)))
    params = lambda mib: pltpu.CompilerParams(vmem_limit_bytes=mib << 20)
    cost = lambda flops: pl.CostEstimate(flops=flops, bytes_accessed=10**6, transcendentals=0)
    table = jnp.asarray(table)
    own, top, bot, pan, table, e1 = pl.pallas_call(
        functools.partial(stage_kernel, count, where, cuts),
        out_shape=[
            VMEM((chunk, 128), F32),
            VMEM((height, 128), F32),
            VMEM((height, 128), F32),
            VMEM((rows, cols), F32),
            VMEM(table.shape, BF16),
            VMEM((LEVELS, rows, cols), F32),
        ],
        in_specs=[pl.BlockSpec(memory_space=pltpu.HBM)] * 3,
        out_specs=[whole] * 6,
        scratch_shapes=[VMEM(multispectral.shape, F32), pltpu.SemaphoreType.DMA((5,))],
        compiler_params=params(8),
        cost_estimate=cost(10**9),
        name="stage",
    )(*in_hbm(multispectral, panchromatic, table))
    q = [own]
    for x, step in zip(packed, steps):
        q.append(lax.ppermute(x, "col", step[0]))
    far = lax.ppermute(far, "row", odd_pairs(row_count))
    sent = lambda corner, rim: -(-(corner + total * rim + -(-total // 4) * rim) // 8) * 8
    a, b, xh = pl.pallas_call(
        functools.partial(rim_kernel, count, low, where),
        out_shape=[shape(height + sent(COEFS, RIM)), shape(sent(8, NEED)), shape(rows)],
        in_specs=[whole] * (3 + count),
        out_specs=[whole] * 3,
        compiler_params=params(8),
        name="rim",
    )(top, bot, table, *q)
    a = lax.ppermute(a, "row", swap_pairs(row_count))
    b = lax.ppermute(b, "row", odd_pairs(row_count))
    smem = pl.BlockSpec(memory_space=pltpu.SMEM)
    part, scaled = pl.pallas_call(
        functools.partial(local_kernel, count, low, where),
        out_shape=[
            jax.ShapeDtypeStruct((total, rows, cols), F32),
            shape(total * BAND_ROWS, 3 * LEVELS * COEFS),
        ],
        in_specs=[smem] + [whole] * (count + 6),
        out_specs=[whole] * 2,
        scratch_shapes=[
            VMEM((rows, 256), F32),
            VMEM((2 * COEFS, cols + 256), F32),
            VMEM((LEVELS, rows, cols), F32),
            VMEM((total * (low + RIM), 256), F32),
            VMEM((total * (low + RIM), cols), F32),
        ],
        compiler_params=params(16),
        cost_estimate=cost(4 * 10**9),
        name="local",
    )(band_gains.T, *q, pan, xh, a, far, pltpu.with_memory_space_constraint(e1, VMEM), table)
    return pl.pallas_call(
        functools.partial(main_kernel, count, bands, where),
        out_shape=jax.ShapeDtypeStruct((total, rows, cols), F32),
        in_specs=[whole] * 4,
        out_specs=pl.BlockSpec(memory_space=pltpu.HBM),
        scratch_shapes=[
            VMEM((total * RIM, 256), F32),
            VMEM((total * RIM, cols), F32),
            VMEM((total, BAND_ROWS, cols), F32),
            pltpu.SemaphoreType.DMA((2, total)),
        ],
        compiler_params=params(16),
        name="combine",
    )(part, scaled, b, table)


def solution(mesh):
    in_specs = (P("col", "row", None), P("row", "col"), P())
    out_specs = P(None, "row", "col")
    return jax.shard_map(
        on_device, mesh=mesh, in_specs=in_specs, out_specs=out_specs, check_vma=False
    )
```

```python
import functools

import jax
import jax.numpy as jnp
import numpy as np
from jax import lax
from jax.experimental import pallas as pl
from jax.experimental.pallas import tpu as pltpu
from jax.sharding import PartitionSpec as P

LEVELS = 3
TAPS = [
    0.2303778133088964,
    0.7148465705529155,
    0.6308807679298587,
    -0.0279837694168599,
    -0.1870348117190931,
    0.0308413818355607,
    0.0328830116668852,
    -0.010597401785069,
]
REACH = 48
COEFS = 24
RIM = 16
NEED = 13
RANK = 21
BAND_ROWS = 56
VMEM = pltpu.VMEM
F32, BF16 = jnp.float32, jnp.bfloat16


def keys_weight(t):
    t = abs(t)
    if t <= 1.0:
        return 1.5 * t**3 - 2.5 * t**2 + 1.0
    return -0.5 * t**3 + 2.5 * t**2 - 4.0 * t + 2.0 if t < 2.0 else 0.0


def upsample_matrix(n):
    m = np.zeros((n, n // 4))
    for y in range(n):
        centre = (y + 0.5) / 4.0 - 0.5
        for k in range(int(np.floor(centre)) - 1, int(np.floor(centre)) + 3):
            m[y, k % (n // 4)] += keys_weight(centre - k)
    return m


def low_matrix(n, tree):
    taps, offset = (TAPS, 3) if tree == 0 else (TAPS[::-1], 4)
    m = np.zeros((n // 2, n))
    for k in range(n // 2):
        for j in range(8):
            m[k, (2 * k + j - offset) % n] += taps[j]
    return m


@functools.lru_cache(None)
def smooth_matrix(n, level):
    total = 0.0
    for tree in range(2):
        chain = np.eye(n)
        for step in range(level):
            chain = low_matrix(n >> step, tree) @ chain
        total = total + 0.5 * chain.T @ chain
    return total


def split_const(m):
    m = np.asarray(m, np.float32)
    hi = m.astype(BF16)
    lo = (m - hi.astype(np.float32)).astype(BF16)
    return hi, lo


@functools.lru_cache(None)
def constants(rows, cols):
    half = cols // 2
    n = 1024
    q = [smooth_matrix(n, level) for level in (1, 2, 3)]
    o = 256
    stack = lambda lo, hi: np.concatenate([m[o : o + 128, lo:hi] for m in q])
    send, recv = [], []
    for lo, hi in ((o - REACH, o), (o + 128, o + 128 + REACH)):
        _, s, vt = np.linalg.svd(stack(lo, hi), full_matrices=False)
        assert s[COEFS - 3] < 1e-14
        send.append(vt[:COEFS])
        recv.append(vt[:COEFS].T)
    below, above = send[0], send[1]
    own, edge = [], ([], [])
    for m in q:
        body = m[o : o + rows]
        own.append(body[:, o : o + rows])
        edge[0].append(body[:REACH, o - REACH : o] @ recv[0])
        edge[1].append(body[-REACH:, o + rows : o + rows + REACH] @ recv[1])
    c1, c2 = [], []
    for m in q:
        body = m[o : o + half]
        c1.append(body[:, o : o + half].T)
        left, right = body[:, o - REACH : o], body[:, o + half : o + half + REACH]
        nothing = np.zeros((half, COEFS))
        first = np.concatenate([left @ recv[0], nothing, right], 1).T
        second = np.concatenate([nothing, right @ recv[1], left], 1).T
        c2.append((first, second))
    qu = q[2] @ upsample_matrix(n)
    p = o // 4
    low = rows // 4
    cu = np.concatenate(
        [
            qu[o : o + cols, p : p + cols // 4],
            qu[o : o + cols, p - RIM : p],
            qu[o : o + cols, p + cols // 4 : p + cols // 4 + RIM],
        ],
        1,
    ).T
    ru = qu[o : o + rows]
    ru_own, ru_rims = ru[:, p : p + low], (ru[:, p - RIM : p], ru[:, p + low : p + low + RIM])
    ru_ends = (ru_rims[0][:BAND_ROWS], ru_rims[1][rows - BAND_ROWS :])
    assert not ru_rims[0][BAND_ROWS:].any() and not ru_rims[1][: rows - BAND_ROWS].any()

    def three(m):
        hi, lo = split_const(m)
        return np.concatenate([hi, hi, lo], 1)

    pair = lambda m: np.concatenate(split_const(m), 1)
    parts = dict(below=pair(below), above=pair(above))
    for level in range(LEVELS):
        parts[f"own{level}"] = pair(own[level])
    for level in range(LEVELS):
        parts[f"c1{level}hi"], parts[f"c1{level}lo"] = split_const(c1[level])
    nothing = np.zeros((REACH, COEFS))
    for level in range(LEVELS):
        parts[f"edge{level}"] = three(np.block([[edge[0][level], nothing], [nothing, edge[1][level]]]))
    for side in range(2):
        parts[f"ru{side}"] = three(np.concatenate([ru_own, ru_rims[side]], 1))
    for side in range(2):
        assert not (ru_rims[0][:, : RIM - NEED] if side == 0 else ru_rims[1][:, NEED:]).any()
        used = ru_ends[side][:, RIM - NEED :] if side == 0 else ru_ends[side][:, :NEED]
        parts[f"end{side}"] = three(np.pad(used, ((0, 0), (0, RIM - NEED))))
        gap = np.zeros((BAND_ROWS - REACH, LEVELS * COEFS))
        m = np.concatenate(edge[side], 1)
        m = np.concatenate([m, gap] if side == 0 else [gap, m])
        for name, x in zip(("fixhi", "fixlo"), split_const(m)):
            parts[f"{name}{side}"] = np.concatenate([x] * 3, 1)
    for level in range(LEVELS):
        for h in range(2):
            parts[f"c2{level}{h}hi"], parts[f"c2{level}{h}lo"] = split_const(c2[level][h])
    for h in range(2):
        parts[f"cu{h}hi"], parts[f"cu{h}lo"] = split_const(cu[:, h * half : (h + 1) * half])
    table, where, at = [], {}, 0
    for name, m in parts.items():
        high = -(-m.shape[0] // 16) * 16
        table.append(np.pad(np.asarray(m, np.float32), ((0, high - m.shape[0]), (0, half - m.shape[1]))))
        where[name] = (at, m.shape)
        at += high
    table = np.concatenate(table).astype(BF16)
    return table, (where["own0"][0], where["edge0"][0]), where


class Table:
    def __init__(self, ref, where):
        self.ref, self.where = ref, where

    def __getitem__(self, name):
        at, (high, wide) = self.where[name]
        return self.ref[at : at + high, 0:wide]

    def pair(self, name):
        x = self[name]
        wide = x.shape[1] // 2
        return x[:, :wide], x[:, wide:]

    def side(self, name, below):
        (first, (high, wide)), (second, _) = self.where[name + "0"], self.where[name + "1"]
        at = pl.multiple_of(jnp.where(below, second, first), 16)
        return self.ref[pl.ds(at, high), 0:wide]

    def two(self, name):
        return self[name + "hi"], self[name + "lo"]


def swap_pairs(count):
    return [(i, i ^ 1) for i in range(count)]


def odd_pairs(count):
    return [(i, (i - 1) % count if i % 2 == 0 else (i + 1) % count) for i in range(count)]


def column_steps(count):
    if count == 4:
        return [
            ([(i, i ^ k) for i in range(4)], k != 2, lambda c, k=k: c ^ k, lambda c, k=k: c ^ k)
            for k in (1, 3, 2)
        ]
    return [
        (
            [(i, (i + k) % count) for i in range(count)],
            k in (1, count - 1),
            lambda c, k=k: lax.rem(c + k, count),
            lambda c, k=k: lax.rem(c + count - k, count),
        )
        for k in [1, count - 1] + list(range(2, count - 1))
    ]


def split(x):
    hi = x.astype(BF16)
    return hi, (x - hi.astype(F32)).astype(BF16)


def dot(a, b, dims=((1,), (0,))):
    return lax.dot_general(a, b, (dims, ((), ())), preferred_element_type=F32)


def dot3(a, b, dims=((1,), (0,))):
    return dot(a[0], b[0], dims) + dot(a[1], b[0], dims) + dot(a[0], b[1], dims)


def rows3(a, b):
    high = a[0].shape[0]
    both = dot(jnp.concatenate(a, 0), b[0])
    return both[:high] + both[high:] + dot(a[0], b[1])


def three_high(x):
    if x.shape[0] % 16:
        hi = x.astype(BF16).astype(F32)
        return jnp.concatenate([hi, x - hi, hi], 0).astype(BF16)
    hi, lo = split(x)
    return jnp.concatenate([hi, lo, hi], 0)


def lanes(shape):
    return lax.broadcasted_iota(jnp.int32, shape, 1)


def pack_chunk(out, ms_ref, to, count):
    bands, low = ms_ref.shape[0], ms_ref.shape[1]
    main = bands * low
    block = lambda k: pl.ds(pl.multiple_of(lax.rem(k + count, count) * 128, 128), 128)
    packed = None
    for i in range(bands):
        out[i * low : (i + 1) * low, :] = ms_ref[i, :, block(to)]
        left, right = ms_ref[i, :, block(to - 1)], ms_ref[i, :, block(to + 1)]
        rim = jnp.where(lanes(left.shape) >= 64, left, right)
        for g in range(low // RIM):
            slot = i * (low // RIM) + g
            rolled = pltpu.roll(rim[g * RIM : (g + 1) * RIM], (2 * RIM * slot + RIM) % 128, 1)
            packed = rolled if slot == 0 else jnp.where(lanes(rolled.shape) >= 2 * RIM * slot, rolled, packed)
    out[main : main + RIM, :] = packed


def pack_kernel(count, where, ms_ref, pan_ref, table_ref, *out_refs):
    c, r = lax.axis_index("col"), lax.axis_index("row")
    table = Table(table_ref, where)
    main = ms_ref.shape[0] * ms_ref.shape[1]
    rows, cols = pan_ref.shape
    below, above = table.pair("below"), table.pair("above")
    choose = lambda first: tuple(
        jnp.where(first, x.astype(F32), y.astype(F32)).astype(BF16) for x, y in zip(below, above)
    )
    for step, out in zip(column_steps(count), out_refs):
        to = step[2](c)
        pack_chunk(out, ms_ref, to, count)
        if step[1]:
            to_right = to == lax.rem(c + 1, count)
            edge = jnp.where(to_right, pltpu.roll(pan_ref[:, cols - 128 :], REACH, 1), pan_ref[:, :128])
            out[main + RIM : main + RIM + COEFS, :] = dot3(choose(to_right), split(edge[:, :REACH]), ((1,), (1,)))
    bottom = lax.rem(r, 2) == 1
    at = pl.multiple_of(jnp.where(bottom, rows - REACH, 0), 16)
    full = dot3(choose(bottom), split(pan_ref[pl.ds(at, REACH), :]))
    for k in range(cols // 128):
        out_refs[-1][k * COEFS : (k + 1) * COEFS, :] = full[:, k * 128 : (k + 1) * 128]


def stage_kernel(count, where, cuts, *refs):
    ms_hbm, pan_hbm, table_hbm = refs[:3]
    own_ref, top_ref, bot_ref, pan_ref, table_ref, e1, ms_ref, sems = refs[3:]
    ends = (0,) + cuts + (table_ref.shape[0],)
    parts = [pl.ds(x, y - x) for x, y in zip(ends, ends[1:])]
    moves = [(pan_hbm, pan_ref)] + [(table_hbm.at[x], table_ref.at[x]) for x in parts[:2]]
    moves += [(ms_hbm, ms_ref), (table_hbm.at[parts[2]], table_ref.at[parts[2]])]
    copies = [pltpu.make_async_copy(x, y, sems.at[k]) for k, (x, y) in enumerate(moves)]
    for copy in copies:
        copy.start()
    copies[0].wait()
    copies[1].wait()
    table = Table(table_ref, where)
    rows, cols = pan_ref.shape
    half = cols // 2
    for out, name, at in ((bot_ref, "below", rows - REACH), (top_ref, "above", 0)):
        full = dot3(table.pair(name), split(pan_ref[at : at + REACH, :]))
        for k in range(cols // 128):
            out[k * COEFS : (k + 1) * COEFS, :] = full[:, k * 128 : (k + 1) * 128]
    copies[2].wait()
    hi, lo = split(pan_ref[...])
    both = jnp.concatenate([hi, lo], 0)
    for level in range(LEVELS):
        t = dot(jnp.concatenate([table.pair(f"own{level}")[0]] * 2, 1), both) + dot(table.pair(f"own{level}")[1], hi)
        main = rows3(split(jnp.concatenate([t[:, :half], t[:, half:]], 0)), table.two(f"c1{level}"))
        e1[level, :, 0:half] = main[:rows]
        e1[level, :, half:] = main[rows:]
    copies[3].wait()
    pack_chunk(own_ref, ms_ref, lax.axis_index("col"), count)
    copies[4].wait()


def rim_kernel(count, low, where, top_ref, bot_ref, table_ref, *refs):
    table = Table(table_ref, where)
    q = refs[:count]
    a_ref, b_ref, xh_ref = refs[count:]
    c, r = lax.axis_index("col"), lax.axis_index("row")
    steps = column_steps(count)
    bands = (q[0].shape[0] - RIM) // low
    main = bands * low
    even = lax.rem(r, 2) == 0
    first = q[1][main + RIM : main + RIM + COEFS, :]
    second = q[2][main + RIM : main + RIM + COEFS, :]
    first_is_right = steps[0][3](c) == lax.rem(c + 1, count)
    left = jnp.where(first_is_right, second, first)
    right = jnp.where(first_is_right, first, second)
    filler = jnp.zeros((128 - 2 * COEFS, 128), F32)
    xh = jnp.concatenate([left, right, filler], 0).T
    xh_ref[...] = xh
    per = low // RIM
    total = count * bands

    def fill(out, bottom, far):
        height = 0 if far else top_ref.shape[0]
        if not far:
            out[0:height, :] = (bot_ref if bottom else top_ref)[...]
        v = table.pair("below" if bottom else "above")
        corner = dot3(v, split(xh[xh.shape[0] - REACH :] if bottom else xh[:REACH]))
        if far:
            tight = jnp.where(lanes(corner.shape) < RANK, corner, pltpu.roll(corner, 128 - (COEFS - RANK), 1))
            packed = tight[0:8]
            for g in (1, 2):
                turned = pltpu.roll(tight[8 * g : 8 * g + 8], 2 * RANK * g, 1)
                packed = jnp.where(lanes(packed.shape) >= 2 * RANK * g, turned, packed)
            out[height : height + 8, :] = packed
        else:
            out[height : height + COEFS, :] = corner
        base = height + (8 if far else COEFS)
        rim_rows = NEED if far else RIM
        packed = None
        for n in range(total):
            ref, i = q[n // bands], n % bands
            row = (i + 1) * low - rim_rows if bottom else i * low
            out[base + n * rim_rows : base + (n + 1) * rim_rows, :] = ref[row : row + rim_rows, :]
            slot = per * (i + 1) - 1 if bottom else per * i
            rim = pltpu.roll(ref[main : main + RIM, :], (2 * RIM * (n % 4 - slot)) % 128, 1)
            packed = rim if n % 4 == 0 else jnp.where(lanes(rim.shape) >= 2 * RIM * (n % 4), rim, packed)
            if n % 4 == 3 or n == total - 1:
                spot = base + total * rim_rows + (n // 4) * rim_rows
                out[spot : spot + rim_rows, :] = packed[RIM - rim_rows :] if bottom else packed[:rim_rows]

    @pl.when(even)
    def _():
        fill(a_ref, 1, False)
        fill(b_ref, 0, True)

    @pl.when(jnp.logical_not(even))
    def _():
        fill(a_ref, 0, False)
        fill(b_ref, 1, True)


def own_rims(own_right, own_left, xh):
    inner = lanes(xh.shape) < 2 * COEFS
    return (
        jnp.where(inner, xh, pltpu.roll(own_right, 2 * COEFS, 1)),
        jnp.where(inner, xh, pltpu.roll(own_left, 2 * COEFS + REACH, 1)),
    )


def low_columns(x_ref, y_ref, table):
    x = split(x_ref[:, 0 : 128 + 2 * RIM])
    half = y_ref.shape[1] // 2
    for h in range(2):
        y_ref[:, h * half : (h + 1) * half] = rows3(x, table.two(f"cu{h}"))


def fill_rows(xe, at, cols, piece, xh):
    blocks = cols // 128
    for k in range(blocks):
        xe[at, k * 128 : (k + 1) * 128] = piece(k)
    f, s = own_rims(piece(blocks // 2), piece(blocks // 2 - 1), xh)
    xe[at, cols : cols + 128] = f
    xe[at, cols + 128 : cols + 256] = s


def coef_piece(ref):
    return lambda k: ref[k * COEFS : (k + 1) * COEFS, :]


def band_rims(mext, ref, total, base, high, skip, rim_rows=RIM):
    filler = [jnp.zeros((RIM - rim_rows, 128), F32)] if rim_rows < RIM else []
    whole = lambda x: jnp.concatenate([x] + filler, 0) if filler else x
    for n in range(total):
        at = slice(n * high + skip, n * high + skip + RIM)
        mext[at, 0:128] = whole(ref[base + n * rim_rows : base + (n + 1) * rim_rows, :])
        spot = base + total * rim_rows + (n // 4) * rim_rows
        mext[at, 128:256] = pltpu.roll(whole(ref[spot : spot + rim_rows, :]), (-2 * RIM * (n % 4)) % 128, 1)


def local_kernel(count, low, where, gains_ref, *refs):
    q, refs = refs[:count], refs[count:]
    pan_ref, xh_ref, a_ref, far_ref, e1, table_ref = refs[:6]
    part_ref, fix_ref, xr, xe, e3, mext, y_ref = refs[6:]
    table = Table(table_ref, where)
    c, r = lax.axis_index("col"), lax.axis_index("row")
    below = lax.rem(r, 2) == 0
    steps = column_steps(count)
    bands = (q[0].shape[0] - RIM) // low
    total = count * bands
    main = bands * low
    rows, cols = pan_ref.shape
    half = cols // 2
    per = low // RIM
    high = low + RIM
    for n in range(total):
        ref, i = q[n // bands], n % bands
        mext[n * high : n * high + low, 0:128] = ref[i * low : (i + 1) * low, :]
        for g in range(per):
            at = n * high + g * RIM
            mext[at : at + RIM, 128:256] = pltpu.roll(
                ref[main : main + RIM, :], (-2 * RIM * (i * per + g)) % 128, 1
            )
    band_rims(mext, a_ref, total, (cols // 128 + 1) * COEFS, high, low)
    low_columns(mext, y_ref, table)
    xr[:, 0:128], xr[:, 128:256] = own_rims(
        pan_ref[:, half : half + 128], pan_ref[:, half - 128 : half], xh_ref[...]
    )
    blocks = cols // 128
    at = lambda under: pl.ds(pl.multiple_of(jnp.where(under, COEFS, 0), 8), COEFS)
    fill_rows(xe, at(below), cols, coef_piece(a_ref), a_ref[blocks * COEFS : (blocks + 1) * COEFS, :])
    fill_rows(xe, at(jnp.logical_not(below)), cols, coef_piece(far_ref), jnp.zeros((COEFS, 128), F32))
    hi, lo = split(xr[...])
    both = jnp.concatenate([hi, lo], 0)
    wide = 2 * COEFS + REACH
    x = xe[...]
    before = [pan_ref[:, h * half : (h + 1) * half] for h in range(2)]
    levels = lambda name: tuple(
        jnp.concatenate([table.two(name(level))[k] for level in range(LEVELS)], 1) for k in range(2)
    )
    high_x = 2 * COEFS
    main_z = rows3(split(jnp.concatenate([x[:, :half], x[:, half:cols]], 0)), levels(lambda level: f"c1{level}"))
    zs = [
        main_z[h * high_x : (h + 1) * high_x]
        + rows3(split(x[:, cols + h * 128 : cols + h * 128 + wide]), levels(lambda level: f"c2{level}{h}"))
        for h in range(2)
    ]
    for level in range(LEVELS):
        ohi, olo = table.pair(f"own{level}")
        t = dot(jnp.concatenate([ohi, ohi], 1), both) + dot(olo, hi)
        for h in range(2):
            z = zs[h][:, level * half : (level + 1) * half]
            hs = slice(h * half, (h + 1) * half)
            de = dot(table[f"edge{level}"], three_high(z))
            e = e1[level, :, hs] + rows3(split(t[:, h * 128 : h * 128 + wide]), table.two(f"c2{level}{h}"))
            e = jnp.concatenate([e[:REACH] + de[:REACH], e[REACH : rows - REACH], e[rows - REACH :] + de[REACH:]], 0)
            e3[level, :, hs] = before[h] - e
            before[h] = e
    far_below = jnp.logical_not(below)
    fix = table.side("fixhi", far_below).astype(F32) + table.side("fixlo", far_below).astype(F32)
    lane = lanes((1, fix.shape[1]))
    level_of = lax.rem(lane, LEVELS * COEFS) // COEFS
    first_two = lanes(fix.shape) < 2 * LEVELS * COEFS
    for j in range(count):
        src = c if j == 0 else steps[j - 1][3](c)
        for i in range(bands):
            n = j * bands + i
            band = src * bands + i
            g1, g2, g3 = gains_ref[0, band], gains_ref[1, band], gains_ref[2, band]
            factor = jnp.where(level_of == 0, g2 - g1, jnp.where(level_of == 1, g3 - g2, -g3))
            scaled = factor * fix
            hi = scaled.astype(BF16).astype(F32)
            fix_ref[n * BAND_ROWS : (n + 1) * BAND_ROWS, :] = jnp.where(first_two, hi, scaled - hi)
            part_ref[n] = (
                dot(table.side("ru", below), three_high(y_ref[n * high : (n + 1) * high, :]))
                + g1 * e3[0]
                + g2 * e3[1]
                + g3 * e3[2]
            )


def main_kernel(count, bands, where, *refs):
    part_ref, fix_ref, b_ref, table_ref, out_ref, mext, y_ref, obuf, sems = refs
    table = Table(table_ref, where)
    c, r = lax.axis_index("col"), lax.axis_index("row")
    steps = column_steps(count)
    below = lax.rem(r, 2) == 1
    total, rows, cols = part_ref.shape
    half = cols // 2
    source = [c if j == 0 else steps[j - 1][3](c) for j in range(count)]
    band = [source[n // bands] * bands + n % bands for n in range(total)]
    done = pl.ds(pl.multiple_of(jnp.where(below, 0, BAND_ROWS), 8), rows - BAND_ROWS)
    late = pl.ds(pl.multiple_of(jnp.where(below, rows - BAND_ROWS, 0), 8), BAND_ROWS)
    copies = [
        pltpu.make_async_copy(part_ref.at[n, done], out_ref.at[band[n], done], sems.at[0, n])
        for n in range(total)
    ]

    @pl.loop(0, total)
    def _(k):
        at = sum(jnp.where(k == n, band[n], 0) for n in range(total))
        pltpu.make_async_copy(part_ref.at[k, done], out_ref.at[at, done], sems.at[0, k]).start()

    band_rims(mext, b_ref, total, 8, RIM, 0, NEED)
    low_columns(mext, y_ref, table)
    packed = b_ref[0:8, :]
    tight = jnp.concatenate([pltpu.roll(packed, (-2 * RANK * g) % 128, 1) for g in range(3)], 0)
    corner = jnp.where(lanes(tight.shape) < COEFS, tight, pltpu.roll(tight, COEFS - RANK, 1))
    corner = split(corner[:, : 2 * COEFS])
    ends = []
    for h in range(2):
        lane = slice(0, 128) if h == 0 else slice(half - 128, half)
        rim = tuple(
            jnp.concatenate([table.two(f"c2{level}{h}")[k][: 2 * COEFS, lane] for level in range(LEVELS)], 1)
            for k in range(2)
        )
        ends.append(dot3(corner, rim))
    stacked = [jnp.concatenate([z[:, level * 128 : (level + 1) * 128] for z in ends], 1) for level in range(LEVELS)]
    fix = dot(fix_ref[...].astype(BF16), three_high(jnp.concatenate(stacked, 0)))
    for n in range(total):
        rim = three_high(y_ref[n * RIM : (n + 1) * RIM, :])
        base = part_ref[n, late, :] + dot(table.side("end", below), rim)
        add = fix[n * BAND_ROWS : (n + 1) * BAND_ROWS]
        obuf[n, :, 0:128] = base[:, 0:128] + add[:, 0:128]
        obuf[n, :, 128 : cols - 128] = base[:, 128 : cols - 128]
        obuf[n, :, cols - 128 :] = base[:, cols - 128 :] + add[:, 128:]
        copy = pltpu.make_async_copy(obuf.at[n], out_ref.at[band[n], late], sems.at[1, n])
        copy.start()
        copies.append(copy)
    for copy in copies:
        copy.wait()


def on_device(multispectral, panchromatic, band_gains):
    count, row_count = lax.axis_size("col"), lax.axis_size("row")
    bands, low, _ = multispectral.shape
    rows, cols = panchromatic.shape
    total = count * bands
    table, cuts, where = constants(rows, cols)
    small = table[: cuts[0]]
    steps = column_steps(count)
    chunk = bands * low + RIM
    shape = lambda n, m=128: jax.ShapeDtypeStruct((n, m), F32)
    whole = pl.BlockSpec(memory_space=VMEM)
    heights = [chunk + (COEFS if step[1] else 0) for step in steps]
    height = cols // 128 * COEFS
    in_hbm = lambda *xs: [pltpu.with_memory_space_constraint(x, pltpu.HBM) for x in xs]
    *packed, far = pl.pallas_call(
        functools.partial(pack_kernel, count, where),
        out_shape=[VMEM((h, 128), F32) for h in heights + [height]],
        grid=(1,),
        in_specs=[
            pl.BlockSpec(multispectral.shape, lambda i: (0, 0, 0)),
            pl.BlockSpec(panchromatic.shape, lambda i: (0, 0)),
            pl.BlockSpec(small.shape, lambda i: (0, 0)),
        ],
        out_specs=[whole] * (len(heights) + 1),
        compiler_params=pltpu.CompilerParams(vmem_limit_bytes=8 << 20),
        name="pack",
    )(*in_hbm(multispectral, panchromatic, jnp.asarray(small)))
    params = lambda mib: pltpu.CompilerParams(vmem_limit_bytes=mib << 20)
    cost = lambda flops: pl.CostEstimate(flops=flops, bytes_accessed=10**6, transcendentals=0)
    table = jnp.asarray(table)
    own, top, bot, pan, table, e1 = pl.pallas_call(
        functools.partial(stage_kernel, count, where, cuts),
        out_shape=[
            VMEM((chunk, 128), F32),
            VMEM((height, 128), F32),
            VMEM((height, 128), F32),
            VMEM((rows, cols), F32),
            VMEM(table.shape, BF16),
            VMEM((LEVELS, rows, cols), F32),
        ],
        in_specs=[pl.BlockSpec(memory_space=pltpu.HBM)] * 3,
        out_specs=[whole] * 6,
        scratch_shapes=[VMEM(multispectral.shape, F32), pltpu.SemaphoreType.DMA((5,))],
        compiler_params=params(8),
        cost_estimate=cost(10**9),
        name="stage",
    )(*in_hbm(multispectral, panchromatic, table))
    q = [own]
    for x, step in zip(packed, steps):
        q.append(lax.ppermute(x, "col", step[0]))
    far = lax.ppermute(far, "row", odd_pairs(row_count))
    sent = lambda corner, rim: -(-(corner + total * rim + -(-total // 4) * rim) // 8) * 8
    a, b, xh = pl.pallas_call(
        functools.partial(rim_kernel, count, low, where),
        out_shape=[shape(height + sent(COEFS, RIM)), shape(sent(8, NEED)), shape(rows)],
        in_specs=[whole] * (3 + count),
        out_specs=[whole] * 3,
        compiler_params=params(8),
        name="rim",
    )(top, bot, table, *q)
    a = lax.ppermute(a, "row", swap_pairs(row_count))
    b = lax.ppermute(b, "row", odd_pairs(row_count))
    smem = pl.BlockSpec(memory_space=pltpu.SMEM)
    part, scaled = pl.pallas_call(
        functools.partial(local_kernel, count, low, where),
        out_shape=[
            jax.ShapeDtypeStruct((total, rows, cols), F32),
            shape(total * BAND_ROWS, 3 * LEVELS * COEFS),
        ],
        in_specs=[smem] + [whole] * (count + 6),
        out_specs=[whole] * 2,
        scratch_shapes=[
            VMEM((rows, 256), F32),
            VMEM((2 * COEFS, cols + 256), F32),
            VMEM((LEVELS, rows, cols), F32),
            VMEM((total * (low + RIM), 256), F32),
            VMEM((total * (low + RIM), cols), F32),
        ],
        compiler_params=params(16),
        cost_estimate=cost(4 * 10**9),
        name="local",
    )(band_gains.T, *q, pan, xh, a, far, pltpu.with_memory_space_constraint(e1, VMEM), table)
    return pl.pallas_call(
        functools.partial(main_kernel, count, bands, where),
        out_shape=jax.ShapeDtypeStruct((total, rows, cols), F32),
        in_specs=[whole] * 4,
        out_specs=pl.BlockSpec(memory_space=pltpu.HBM),
        scratch_shapes=[
            VMEM((total * RIM, 256), F32),
            VMEM((total * RIM, cols), F32),
            VMEM((total, BAND_ROWS, cols), F32),
            pltpu.SemaphoreType.DMA((2, total)),
        ],
        compiler_params=params(16),
        name="combine",
    )(part, scaled, b, table)


def solution(mesh):
    in_specs = (P("col", "row", None), P("row", "col"), P())
    out_specs = P(None, "row", "col")
    return jax.shard_map(
        on_device, mesh=mesh, in_specs=in_specs, out_specs=out_specs, check_vma=False
    )
```
